32 devices in a mesh: row: 4 (over y, x), col: 8 (over z, core).
Axes of the slice: x: 2, y: 2, z: 4, core: 2. Of those that a mesh axis runs over, the one named last changes fastest.
Arguments:
- pixels_tokens: bfloat16 [4, 2304, 5120], P(None, 'col', 'row'), may hold values from -12 to 12, as said below
- ln_gain: float32 [5120], replicated, may hold values from 0.1 to 1.9
- ln_bias: float32 [5120], replicated, may hold values from -3 to 3
- w_qkv: bfloat16 [5120, 6144], P('col', 'row'), may hold values from -1 to 1, as said below
- w_out: bfloat16 [2048, 5120], P('col', 'row'), may hold values from -0.125 to 0.125
Outputs:
- block_out: bfloat16 [4, 2304, 5120], P(None, 'col', 'row')
The draws below stay inside these ranges and needn't reach their ends.
Inputs may be any that keep to these rules, and one draw needn't show every extreme that they name: `pixels_tokens`: activations of order one. `w_qkv`: projection entries scaled by the width.
All inputs are finite; a program needn't handle non-finite values.
Results may differ from the reference program's by a relative error of at most 0.012.
The reference program's roundings to bfloat16 on the way (of `normed`, `qkv`, `weights` and `heads_out`) count: a program that leaves them out, or rounds other values in their place, can miss the bound.
Values may be sent and summed in bfloat16 or wider, within the bound.
No kernel may reach another device: no remote copies, remote signals or barrier semaphores. Data moves between devices by JAX's collectives and lax.ppermute only.
A program may use at most 128 MiB of HBM per device.

```python
import jax
import jax.numpy as jnp
from jax import lax

D = 5120
HDIM = 128
SEQ = 2304
IMAGES = 4
HEADS = 16


def draw_pixels_tokens(key, part):
    values = jax.random.normal(jax.random.fold_in(key, 1), (IMAGES, SEQ, D), jnp.float32)
    return jnp.clip(values, -12.0, 12.0).astype(jnp.bfloat16)


def draw_w_qkv(key, part):
    weights = jax.random.normal(jax.random.fold_in(key, 3), (D, HEADS * 3 * HDIM), jnp.float32) * (2.0 / jnp.sqrt(float(D)))
    return jnp.clip(weights, -1.0, 1.0).astype(jnp.bfloat16)


def shard_levels(own_key, extent, pieces, low, high):
    level, own = 1.0, jax.random.fold_in(own_key, 6)
    for position, parts in pieces:
        draws = jnp.exp(jax.random.uniform(jax.random.fold_in(own, position), (parts,), jnp.float32, low / len(pieces), high / len(pieces)))
        level = level * jnp.repeat(draws, extent[position] // parts).reshape([-1 if axis == position else 1 for axis in range(len(extent))])
    return level


def scatter_about(rng, dims, scale, limit, pieces=(), held_as=jnp.bfloat16):
    level = shard_levels(rng, dims, pieces, -0.22, 0.18) if pieces else 1.0
    drawn = jax.random.normal(rng, dims, jnp.float32) * scale * level
    return jnp.minimum(jnp.maximum(drawn, -limit), limit).astype(held_as)


def setup_inputs(seed: int = 0) -> dict:
    key_of = jax.random.split(jax.random.key(seed), 6)
    pixels_tokens = draw_pixels_tokens(jax.random.fold_in(key_of[5], 71), 0)
    ln_gain = jnp.clip(1.0 + 0.18 * jax.random.normal(key_of[1], (D,), jnp.float32), 0.1, 1.9)
    ln_bias = scatter_about(key_of[2], (D,), 0.5, 3.0, (), jnp.float32)
    w_qkv = draw_w_qkv(jax.random.fold_in(key_of[5], 71), 0)
    w_out = scatter_about(key_of[4], (HEADS * HDIM, D), (HEADS * HDIM) ** -0.5, 0.125, ((0, 8), (1, 4)))
    return {"pixels_tokens": pixels_tokens, "ln_gain": ln_gain, "ln_bias": ln_bias, "w_qkv": w_qkv, "w_out": w_out}


def layer_norm(values, ln_gain, ln_bias):
    floats = values.astype(jnp.float32)
    center = lax.optimization_barrier(jnp.mean(floats, axis=-1, keepdims=True))
    spread = lax.optimization_barrier(jnp.mean((floats - center) * (floats - center), axis=-1, keepdims=True))
    return ((floats - center) * lax.rsqrt(spread + 1e-06) * ln_gain + ln_bias).astype(jnp.bfloat16)

def attend(triple):
    query, keys, values = (triple[0], triple[1], triple[2])
    scores = jnp.dot(query, keys.T, preferred_element_type=jnp.float32) * HDIM ** (-0.5)
    peak = lax.optimization_barrier(jnp.max(scores, axis=-1, keepdims=True))
    expo = jnp.exp(scores - peak)
    weights = (expo / lax.optimization_barrier(jnp.sum(expo, axis=-1, keepdims=True))).astype(jnp.bfloat16)
    return jnp.dot(weights, values, preferred_element_type=jnp.float32).astype(jnp.bfloat16)

def reference(pixels_tokens, ln_gain, ln_bias, w_qkv, w_out):
    normed = layer_norm(pixels_tokens, ln_gain, ln_bias).reshape(IMAGES * SEQ, D)
    qkv = jnp.dot(normed, w_qkv, preferred_element_type=jnp.float32).astype(jnp.bfloat16)
    qkv = qkv.reshape(IMAGES, SEQ, HEADS, 3, HDIM).transpose(0, 2, 3, 1, 4).reshape(IMAGES * HEADS, 3, SEQ, HDIM)
    heads_out = lax.map(attend, qkv)
    heads_out = heads_out.reshape(IMAGES, HEADS, SEQ, HDIM).transpose(0, 2, 1, 3).reshape(IMAGES * SEQ, HEADS * HDIM)
    projected = jnp.dot(heads_out, w_out, preferred_element_type=jnp.float32)
    summed = pixels_tokens.reshape(IMAGES * SEQ, D).astype(jnp.float32) + projected
    return summed.astype(jnp.bfloat16).reshape(IMAGES, SEQ, D)
```

```python
import functools

import jax
import jax.numpy as jnp
from jax import lax
from jax.experimental import pallas as pl
from jax.experimental.pallas import tpu as pltpu
from jax.sharding import PartitionSpec as P

HDIM = 128
CHUNKS = (2, 2)
ANY = pl.BlockSpec(memory_space=pl.ANY)
VMEM = pl.BlockSpec(memory_space=pltpu.VMEM)


def ring(images, parts, step):
    return [
        (a * parts + b, ((a + step) % images) * parts + b)
        for a in range(images)
        for b in range(parts)
    ]


def group(images, parts, step):
    return [
        (a * parts + b, a * parts + (b + step) % parts)
        for a in range(images)
        for b in range(parts)
    ]


def tile_of(rows, limit):
    return max(t for t in range(16, limit + 1, 16) if rows % t == 0)


def spread(block, rows, dims):
    pieces = [(0, block)]
    for d in dims:
        perm = [(a, a ^ d) for a in range(rows)]
        pieces += [(m ^ d, lax.ppermute(b, "row", perm)) for m, b in pieces]
    return pieces


def norm_kernel(masks, gain_ref, bias_ref, *refs):
    pieces, out_ref = refs[:-1], refs[-1]
    me = lax.axis_index("row")
    width = pieces[0].shape[1]
    total = width * len(pieces)
    floats = [ref[...].astype(jnp.float32) for ref in pieces]
    center = sum(jnp.sum(f, axis=-1, keepdims=True) for f in floats) / total
    floats = [f - center for f in floats]
    spread_ = sum(jnp.sum(f * f, axis=-1, keepdims=True) for f in floats) / total
    scale = lax.rsqrt(spread_ + 1e-06)
    for mask, f in zip(masks, floats):
        at = pl.ds(pl.multiple_of((me ^ mask) * width, 128), width)
        out_ref[:, at] = (f * scale * gain_ref[:, at] + bias_ref[:, at]).astype(out_ref.dtype)


def normalize(pieces, gain, bias):
    masks = [m for m, _ in pieces]
    rows, width = pieces[0][1].shape
    total = width * len(pieces)
    tile = tile_of(rows, 96)
    whole = pl.BlockSpec((1, total), lambda t: (0, 0))
    return pl.pallas_call(
        functools.partial(norm_kernel, masks),
        grid=(rows // tile,),
        in_specs=[whole, whole] + [pl.BlockSpec((tile, width), lambda t: (t, 0))] * len(pieces),
        out_specs=pl.BlockSpec((tile, total), lambda t: (t, 0)),
        out_shape=jax.ShapeDtypeStruct((rows, total), jnp.bfloat16),
        cost_estimate=pl.CostEstimate(
            flops=8 * rows * total, bytes_accessed=4 * rows * total, transcendentals=rows
        ),
        name="norm",
    )(gain[None], bias[None], *[b for _, b in pieces])


def place(images, parts, step, turn):
    mine = lax.axis_index("col")
    image, part = mine // parts, mine % parts
    return ((image + images - step) % images) * parts + (part + parts - turn) % parts


def qkv_kernel(images, parts, heads, tags, *refs):
    x_refs = refs[:images]
    w_refs = refs[images : images + len(tags)]
    q_ref, kv_ref, x_v, w_v, x_sem, w_sem = refs[images + len(tags) :]
    depth = w_refs[0].shape[0]
    rows = x_refs[0].shape[0]
    copies = []
    for n, (step, turn) in enumerate(tags):
        at = pl.multiple_of(place(images, parts, step, turn) * depth, 16)
        copies.append(pltpu.make_async_copy(w_refs[n], w_v.at[pl.ds(at, depth)], w_sem.at[n]))
    loads = [pltpu.make_async_copy(x_refs[k], x_v.at[k], x_sem.at[k]) for k in range(images)]
    for copy in copies:
        copy.start()
    for load in loads:
        load.start()
    for copy in copies:
        copy.wait()
    for k in range(images):
        loads[k].wait()
        got = jnp.dot(x_v[k], w_v[...], preferred_element_type=jnp.float32).astype(jnp.bfloat16)
        own = pl.ds(k * rows, rows)
        for h in range(heads):
            at = 3 * HDIM * h
            q_ref[own, h * HDIM : (h + 1) * HDIM] = got[:, at : at + HDIM]
            kv_ref[own, 2 * h * HDIM : 2 * (h + 1) * HDIM] = got[:, at + HDIM : at + 3 * HDIM]


def project_qkv(blocks, pieces, images, parts, heads):
    rows, total = blocks[0].shape
    columns = pieces[0][2].shape[1]
    tags = [(s, t) for s, t, _ in pieces]
    tokens = images * rows
    return pl.pallas_call(
        functools.partial(qkv_kernel, images, parts, heads, tags),
        in_specs=[ANY] * (images + len(pieces)),
        out_specs=[VMEM, VMEM],
        out_shape=[
            jax.ShapeDtypeStruct((tokens, heads * HDIM), jnp.bfloat16),
            jax.ShapeDtypeStruct((tokens, 2 * heads * HDIM), jnp.bfloat16),
        ],
        scratch_shapes=[
            pltpu.VMEM((images, rows, total), jnp.bfloat16),
            pltpu.VMEM((total, columns), jnp.bfloat16),
            pltpu.SemaphoreType.DMA((images,)),
            pltpu.SemaphoreType.DMA((len(pieces),)),
        ],
        cost_estimate=pl.CostEstimate(
            flops=2 * tokens * total * columns,
            bytes_accessed=2 * (tokens * total + total * columns + tokens * columns),
            transcendentals=0,
        ),
        name="qkv",
    )(*blocks, *[w for _, _, w in pieces])


def attend_kernel(images, heads, tile, q_ref, *refs):
    kv_refs, out_refs = refs[:-images], refs[-images:]
    rows = out_refs[0].shape[0]
    scale = HDIM ** (-0.5)
    for h in range(heads):
        keys = [ref[:, 2 * h * HDIM : (2 * h + 1) * HDIM] for ref in kv_refs]
        values = [ref[:, (2 * h + 1) * HDIM : 2 * (h + 1) * HDIM] for ref in kv_refs]
        for k in range(images):

            def step(n, carry, h=h, k=k, keys=keys, values=values):
                at = pl.multiple_of(n * tile, 16)
                query = q_ref[pl.ds(k * rows + at, tile), h * HDIM : (h + 1) * HDIM]
                scores = [
                    lax.dot_general(
                        query, key, (((1,), (1,)), ((), ())), preferred_element_type=jnp.float32
                    )
                    * scale
                    for key in keys
                ]
                peak = functools.reduce(
                    jnp.maximum, [jnp.max(s, axis=-1, keepdims=True) for s in scores]
                )
                expo = [jnp.exp(s - peak) for s in scores]
                inverse = 1.0 / sum(jnp.sum(e, axis=-1, keepdims=True) for e in expo)
                got = sum(
                    jnp.dot(
                        (e * inverse).astype(jnp.bfloat16), value, preferred_element_type=jnp.float32
                    )
                    for e, value in zip(expo, values)
                )
                out_refs[k][pl.ds(at, tile), h * HDIM : (h + 1) * HDIM] = got.astype(jnp.bfloat16)
                return carry

            lax.fori_loop(0, rows // tile, step, 0)


def attend(query, pairs, images, heads):
    tokens = query.shape[0]
    rows = tokens // images
    keys = tokens * len(pairs)
    return pl.pallas_call(
        functools.partial(attend_kernel, images, heads, tile_of(rows, 144)),
        in_specs=[VMEM] * (1 + len(pairs)),
        out_specs=[VMEM] * images,
        out_shape=[jax.ShapeDtypeStruct((rows, heads * HDIM), jnp.bfloat16)] * images,
        cost_estimate=pl.CostEstimate(
            flops=8 * heads * tokens * keys * HDIM,
            bytes_accessed=4 * heads * HDIM * (tokens + keys),
            transcendentals=heads * tokens * keys,
        ),
        name="attend",
    )(query, *pairs)


def out_kernel(images, parts, head_row, spans, o_tags, w_tags, last, *refs):
    o_refs = refs[: len(o_tags)]
    refs = refs[len(o_tags) :]
    w_refs = refs[: len(w_tags)]
    base_ref, out_ref, o_v, w_v, o_sem, w_sem = refs[len(w_tags) :]
    me = lax.axis_index("row")
    depth = w_refs[0].shape[0]
    image = lax.axis_index("col") // parts
    width = o_v.shape[2]
    copies = []
    for n, (step, turn) in enumerate(w_tags):
        at = pl.multiple_of(place(images, parts, step, turn) * depth, 16)
        copies.append(pltpu.make_async_copy(w_refs[n], w_v.at[pl.ds(at, depth)], w_sem.at[n]))
    loads = []
    for n, (first, mask) in enumerate(o_tags):
        loads.append(
            pltpu.make_async_copy(
                o_refs[n], o_v.at[me ^ mask, pl.ds(first, o_refs[n].shape[0])], o_sem.at[n]
            )
        )
    for copy in copies + loads:
        copy.start()
    for copy in copies + loads:
        copy.wait()
    begin, count = spans
    rows = out_ref.shape[1]
    for k in range(images):
        at = (image + k) % images
        o_all = jnp.concatenate(
            [o_v[r, k * rows : (k + 1) * rows, :] for r in range(o_v.shape[0])], axis=1
        )
        w_all = jnp.concatenate(
            [
                w_v[(r * head_row + begin) * HDIM : (r * head_row + begin + count) * HDIM, :]
                for r in range(o_v.shape[0])
            ],
            axis=0,
        )
        got = jnp.dot(o_all, w_all, preferred_element_type=jnp.float32)
        out_ref[at] = (base_ref[at].astype(jnp.float32) + got).astype(out_ref.dtype)


def project_out(base, o_pieces, w_pieces, images, parts, head_row, rows_count, spans, last):
    o_tags = [(f, m) for f, m, _ in o_pieces]
    w_tags = [(s, t) for s, t, _ in w_pieces]
    count, rows, columns = base.shape
    width = o_pieces[0][2].shape[1]
    deep = len(w_pieces) * w_pieces[0][2].shape[0]
    kind = jnp.bfloat16 if last else jnp.float32
    return pl.pallas_call(
        functools.partial(out_kernel, images, parts, head_row, spans, o_tags, w_tags, last),
        in_specs=[ANY] * (len(o_tags) + len(w_tags)) + [VMEM],
        out_specs=VMEM,
        out_shape=jax.ShapeDtypeStruct(base.shape, kind),
        scratch_shapes=[
            pltpu.VMEM((rows_count, count * rows, width), jnp.bfloat16),
            pltpu.VMEM((deep, columns), jnp.bfloat16),
            pltpu.SemaphoreType.DMA((len(o_tags),)),
            pltpu.SemaphoreType.DMA((len(w_tags),)),
        ],
        cost_estimate=pl.CostEstimate(
            flops=2 * count * rows * columns * width * rows_count,
            bytes_accessed=8 * count * rows * columns,
            transcendentals=0,
        ),
        name="out",
    )(*[o for _, _, o in o_pieces], *[w for _, _, w in w_pieces], base)


def local(pixels_tokens, ln_gain, ln_bias, w_qkv, w_out):
    images, rows, width = pixels_tokens.shape
    row_count = lax.axis_size("row")
    col_count = lax.axis_size("col")
    parts = col_count // images
    head_row = w_qkv.shape[1] // (3 * HDIM)
    image = lax.axis_index("col") // parts
    dims = [1 << n for n in range(row_count.bit_length() - 1)]

    def around(value, step):
        return lax.ppermute(value, "col", ring(images, parts, step)) if step % images else value

    def gather_col(shard):
        pieces = []
        for step in range(images):
            pieces.append((step, 0, shard))
            for turn in range(1, parts):
                pieces.append((step, turn, lax.ppermute(shard, "col", group(images, parts, turn))))
            if step + 1 < images:
                shard = around(shard, 1)
        return pieces

    blocks = []
    for k in range(images):
        block = lax.dynamic_index_in_dim(pixels_tokens, (image + k) % images, 0, keepdims=False)
        blocks.append(around(block, k))
    normed = []
    for k in range(images):
        turned = dims[k % len(dims) :] + dims[: k % len(dims)]
        normed.append(normalize(spread(blocks[k], row_count, turned), ln_gain, ln_bias))

    begin = 0
    results = []
    for heads in CHUNKS:
        own = w_qkv[:, begin * 3 * HDIM : (begin + heads) * 3 * HDIM]
        query, pair = project_qkv(normed, gather_col(own), images, parts, heads)
        pairs = [pair] + [
            lax.ppermute(pair, "col", group(images, parts, turn)) for turn in range(1, parts)
        ]
        outs = attend(query, pairs, images, heads)
        outs = [around(o, -k) for k, o in enumerate(outs)]
        half = images // 2
        pieces = []
        for n in range(2):
            joined = jnp.concatenate(outs[n * half : (n + 1) * half], axis=0)
            turned = dims[n:] + dims[:n]
            pieces += [(n * half * rows, m, b) for m, b in spread(joined, row_count, turned)]
        results.append(((begin, heads), pieces))
        begin += heads

    out_pieces = gather_col(w_out)
    total = pixels_tokens
    for n, (spans, pieces) in enumerate(results):
        total = project_out(
            total, pieces, out_pieces, images, parts, head_row, row_count, spans, n + 1 == len(results)
        )
    return total


def solution(mesh):
    in_specs = (P(None, "col", "row"), P(), P(), P("col", "row"), P("col", "row"))
    out_specs = P(None, "col", "row")
    return jax.shard_map(local, mesh=mesh, in_specs=in_specs, out_specs=out_specs, check_vma=False)
```

```python
import functools

import jax
import jax.numpy as jnp
from jax import lax
from jax.experimental import pallas as pl
from jax.experimental.pallas import tpu as pltpu
from jax.sharding import PartitionSpec as P

HDIM = 128
CHUNKS = 2
ANY = pl.BlockSpec(memory_space=pl.ANY)
VMEM = pl.BlockSpec(memory_space=pltpu.VMEM)


def ring(images, parts, step):
    return [
        (a * parts + b, ((a + step) % images) * parts + b)
        for a in range(images)
        for b in range(parts)
    ]


def group(images, parts, step):
    return [
        (a * parts + b, a * parts + (b + step) % parts)
        for a in range(images)
        for b in range(parts)
    ]


def tile_of(rows, limit):
    return max(t for t in range(16, limit + 1, 16) if rows % t == 0)


def cost(flops, moved, exps=0):
    return pl.CostEstimate(flops=flops, bytes_accessed=moved, transcendentals=exps)


def spread(block, rows, dims):
    pieces, n = [(0, block)], 0
    for d in dims:
        perm = [(a, a ^ d) for a in range(rows)]
        for m, b in list(pieces):
            pieces.append((m ^ d, lax.ppermute(b, "row", perm)))
            n += 1
    return pieces


def norm_kernel(masks, images, parts, gain_ref, bias_ref, *refs):
    pieces, out_ref = refs[: len(masks)], refs[-1]
    me = lax.axis_index("row")
    image = lax.axis_index("col") // parts
    width = pieces[0].shape[1]
    span = out_ref.shape[3]
    grain = min(width, span)
    total = width * len(pieces)
    floats = [ref[...].astype(jnp.float32) for ref in pieces]
    center = sum(jnp.sum(f, axis=-1, keepdims=True) for f in floats) / total
    floats = [f - center for f in floats]
    scatter = sum(jnp.sum(f * f, axis=-1, keepdims=True) for f in floats) / total
    scale = lax.rsqrt(scatter + 1e-06)
    for mask, f in zip(masks, floats):
        for part in range(width // grain):
            first = (me ^ mask) * width + part * grain
            at = pl.ds(pl.multiple_of(first, 128), grain)
            step = (image + images - first // span) % images
            to = pl.ds(pl.multiple_of(first % span, 128), grain)
            value = f[:, part * grain : (part + 1) * grain] * scale
            out_ref[0, step, :, to] = (value * gain_ref[:, at] + bias_ref[:, at]).astype(
                out_ref.dtype
            )


def normalize(k, held, pieces, gain, bias, images, parts):
    masks = [m for m, _ in pieces]
    rows, width = pieces[0][1].shape
    total = width * len(pieces)
    tile = tile_of(rows, 48)
    shape = (images, images, rows, total // images)
    whole = pl.BlockSpec((1, total), lambda t: (0, 0))
    extra = [] if held is None else [held]
    return pl.pallas_call(
        functools.partial(norm_kernel, masks, images, parts),
        grid=(rows // tile,),
        in_specs=[whole, whole]
        + [pl.BlockSpec((tile, width), lambda t: (t, 0))] * len(pieces)
        + [ANY] * len(extra),
        out_specs=pl.BlockSpec((1, images, tile, total // images), lambda t: (k, 0, t, 0)),
        out_shape=jax.ShapeDtypeStruct(shape, jnp.bfloat16),
        input_output_aliases={2 + len(pieces): 0} if extra else {},
        cost_estimate=cost(8 * rows * total, 4 * rows * total, rows),
        name="norm",
    )(gain[None], bias[None], *[b for _, b in pieces], *extra)


def piece_copies(w_refs, tags, parts, w_v, sems):
    part = lax.axis_index("col") % parts
    copies = []
    for n, (step, turn) in enumerate(tags):
        depth = w_refs[n].shape[0]
        at = pl.multiple_of(((part + parts - turn) % parts) * depth, 16)
        copies.append(
            pltpu.make_async_copy(w_refs[n], w_v.at[pl.ds(step * parts * depth + at, depth)], sems.at[n])
        )
    return copies


def early_kernel(steps, parts, tags, x_ref, *refs):
    w_refs = refs[: len(tags)]
    out_ref, x_v, w_v, o_v, x_sem, w_sem, o_sem = refs[len(tags) :]
    images, _, _, span = x_ref.shape
    half = w_v.shape[1] // CHUNKS
    copies = piece_copies(w_refs, tags, parts, w_v, w_sem)
    loads = [
        [
            pltpu.make_async_copy(
                x_ref.at[k, s], x_v.at[k, :, pl.ds(s * span, span)], x_sem.at[k, s]
            )
            for s in range(steps)
        ]
        for k in range(images)
    ]
    for copy in copies:
        copy.start()
    for block in loads:
        for load in block:
            load.start()
    for copy in copies:
        copy.wait()
    stores = []
    for k in range(images):
        for load in loads[k]:
            load.wait()
        for n in range(CHUNKS):
            m = k * CHUNKS + n
            slot = m % 2
            if m >= 2:
                stores[m - 2].wait()
            o_v[slot] = jnp.dot(
                x_v[k], w_v[:, n * half : (n + 1) * half], preferred_element_type=jnp.float32
            )
            store = pltpu.make_async_copy(o_v.at[slot], out_ref.at[n, k], o_sem.at[slot])
            store.start()
            stores.append(store)
    for store in stores[-2:]:
        store.wait()


def project_early(normed, pieces, parts):
    images, _, rows, span = normed.shape
    columns = pieces[0][2].shape[1]
    tags = [(s, t) for s, t, _ in pieces]
    steps = images - 1
    half = columns // CHUNKS
    tokens = images * rows
    return pl.pallas_call(
        functools.partial(early_kernel, steps, parts, tags),
        in_specs=[ANY] * (1 + len(pieces)),
        out_specs=ANY,
        out_shape=jax.ShapeDtypeStruct((CHUNKS, images, rows, half), jnp.float32),
        scratch_shapes=[
            pltpu.VMEM((images, rows, steps * span), jnp.bfloat16),
            pltpu.VMEM((steps * span, columns), jnp.bfloat16),
            pltpu.VMEM((2, rows, half), jnp.float32),
            pltpu.SemaphoreType.DMA((images, steps)),
            pltpu.SemaphoreType.DMA((len(pieces),)),
            pltpu.SemaphoreType.DMA((2,)),
        ],
        cost_estimate=cost(2 * tokens * steps * span * columns, 2 * tokens * span * steps),
        name="early",
    )(normed, *[w for _, _, w in pieces])


def late_kernel(chunk, parts, heads, tags, x_ref, acc_ref, *refs):
    w_refs = refs[: len(tags)]
    q_ref, kv_ref, x_v, a_v, w_v, x_sem, a_sem, w_sem = refs[len(tags) :]
    images, _, rows, _ = x_ref.shape
    copies = piece_copies(w_refs, [(0, t) for _, t in tags], parts, w_v, w_sem)
    loads = [
        (
            pltpu.make_async_copy(x_ref.at[k, images - 1], x_v.at[k], x_sem.at[k]),
            pltpu.make_async_copy(acc_ref.at[chunk, k], a_v.at[k], a_sem.at[k]),
        )
        for k in range(images)
    ]
    for copy in copies:
        copy.start()
    for pair in loads:
        for load in pair:
            load.start()
    for copy in copies:
        copy.wait()
    for k in range(images):
        for load in loads[k]:
            load.wait()
        got = a_v[k] + jnp.dot(x_v[k], w_v[...], preferred_element_type=jnp.float32)
        got = got.astype(jnp.bfloat16)
        own = pl.ds(k * rows, rows)
        for h in range(heads):
            at = 3 * HDIM * h
            q_ref[own, h * HDIM : (h + 1) * HDIM] = got[:, at : at + HDIM]
            kv_ref[own, 2 * h * HDIM : 2 * (h + 1) * HDIM] = got[:, at + HDIM : at + 3 * HDIM]


def project_late(chunk, normed, acc, pieces, parts):
    images, _, rows, span = normed.shape
    columns = pieces[0][2].shape[1]
    heads = columns // (3 * HDIM)
    tags = [(s, t) for s, t, _ in pieces]
    tokens = images * rows
    return pl.pallas_call(
        functools.partial(late_kernel, chunk, parts, heads, tags),
        in_specs=[ANY] * (2 + len(pieces)),
        out_specs=[VMEM, VMEM],
        out_shape=[
            jax.ShapeDtypeStruct((tokens, heads * HDIM), jnp.bfloat16),
            jax.ShapeDtypeStruct((tokens, 2 * heads * HDIM), jnp.bfloat16),
        ],
        scratch_shapes=[
            pltpu.VMEM((images, rows, span), jnp.bfloat16),
            pltpu.VMEM((images, rows, columns), jnp.float32),
            pltpu.VMEM((span, columns), jnp.bfloat16),
            pltpu.SemaphoreType.DMA((images,)),
            pltpu.SemaphoreType.DMA((images,)),
            pltpu.SemaphoreType.DMA((len(pieces),)),
        ],
        cost_estimate=cost(2 * tokens * span * columns, 8 * tokens * columns),
        name="late",
    )(normed, acc, *[w for _, _, w in pieces])


def attend_kernel(images, heads, q_ref, *refs):
    kv_refs, out_refs = refs[:-images], refs[-images:]
    rows = out_refs[0].shape[0]
    scale = HDIM ** (-0.5)

    def block(k, carry):
        own = pl.ds(pl.multiple_of(k * rows, 16), rows)
        for h in range(heads):
            query = q_ref[own, h * HDIM : (h + 1) * HDIM]
            scores = [
                lax.dot_general(
                    query,
                    ref[:, 2 * h * HDIM : (2 * h + 1) * HDIM],
                    (((1,), (1,)), ((), ())),
                    preferred_element_type=jnp.float32,
                )
                * scale
                for ref in kv_refs
            ]
            peak = functools.reduce(
                jnp.maximum, [jnp.max(s, axis=-1, keepdims=True) for s in scores]
            )
            expo = [jnp.exp(s - peak) for s in scores]
            inverse = 1.0 / sum(jnp.sum(e, axis=-1, keepdims=True) for e in expo)
            got = sum(
                jnp.dot(
                    (e * inverse).astype(jnp.bfloat16),
                    ref[:, (2 * h + 1) * HDIM : 2 * (h + 1) * HDIM],
                    preferred_element_type=jnp.float32,
                )
                for e, ref in zip(expo, kv_refs)
            ).astype(jnp.bfloat16)
            for n in range(images):

                @pl.when(k == n)
                def _(n=n, h=h, got=got):
                    out_refs[n][:, h * HDIM : (h + 1) * HDIM] = got

        return carry

    lax.fori_loop(0, images, block, 0)


def attend(query, pairs, images):
    tokens, wide = query.shape
    rows, heads = tokens // images, wide // HDIM
    keys = tokens * len(pairs)
    return pl.pallas_call(
        functools.partial(attend_kernel, images, heads),
        in_specs=[VMEM] * (1 + len(pairs)),
        out_specs=[VMEM] * images,
        out_shape=[jax.ShapeDtypeStruct((rows, wide), jnp.bfloat16)] * images,
        cost_estimate=cost(
            8 * heads * tokens * keys * HDIM,
            4 * heads * HDIM * (tokens + keys),
            heads * tokens * keys,
        ),
        name="attend",
    )(query, *pairs)


def out_kernel(images, parts, head_row, begin, count, o_tags, w_tags, *refs):
    o_refs = refs[: len(o_tags)]
    refs = refs[len(o_tags) :]
    w_refs = refs[: len(w_tags)]
    base_ref, out_ref, o_v, w_v, o_sem, w_sem = refs[len(w_tags) :]
    me = lax.axis_index("row")
    col = lax.axis_index("col")
    image, part = col // parts, col % parts
    depth = w_refs[0].shape[0]
    copies = []
    for n, (step, turn) in enumerate(w_tags):
        place = ((image + images - step) % images) * parts + (part + parts - turn) % parts
        at = pl.multiple_of(place * depth, 16)
        copies.append(pltpu.make_async_copy(w_refs[n], w_v.at[pl.ds(at, depth)], w_sem.at[n]))
    for n, (first, mask) in enumerate(o_tags):
        to = o_v.at[me ^ mask, pl.ds(first, o_refs[n].shape[0])]
        copies.append(pltpu.make_async_copy(o_refs[n], to, o_sem.at[n]))
    for copy in copies:
        copy.start()
    for copy in copies:
        copy.wait()
    rows = out_ref.shape[1]
    w_all = jnp.concatenate(
        [
            w_v[(r * head_row + begin) * HDIM : (r * head_row + begin + count) * HDIM, :]
            for r in range(o_v.shape[0])
        ],
        axis=0,
    )
    for k in range(images):
        at = (image + k) % images
        o_all = jnp.concatenate(
            [o_v[r, k * rows : (k + 1) * rows, :] for r in range(o_v.shape[0])], axis=1
        )
        got = jnp.dot(o_all, w_all, preferred_element_type=jnp.float32)
        out_ref[at] = (base_ref[at].astype(jnp.float32) + got).astype(out_ref.dtype)


def project_out(base, o_pieces, w_pieces, parts, head_row, row_count, begin, kind):
    o_tags = [(f, m) for f, m, _ in o_pieces]
    w_tags = [(s, t) for s, t, _ in w_pieces]
    images, rows, columns = base.shape
    width = o_pieces[0][2].shape[1]
    deep = len(w_pieces) * w_pieces[0][2].shape[0]
    return pl.pallas_call(
        functools.partial(
            out_kernel, images, parts, head_row, begin, width // HDIM, o_tags, w_tags
        ),
        in_specs=[ANY] * (len(o_tags) + len(w_tags)) + [VMEM],
        out_specs=VMEM,
        out_shape=jax.ShapeDtypeStruct(base.shape, kind),
        scratch_shapes=[
            pltpu.VMEM((row_count, images * rows, width), jnp.bfloat16),
            pltpu.VMEM((deep, columns), jnp.bfloat16),
            pltpu.SemaphoreType.DMA((len(o_tags),)),
            pltpu.SemaphoreType.DMA((len(w_tags),)),
        ],
        cost_estimate=cost(
            2 * images * rows * columns * width * row_count, 8 * images * rows * columns
        ),
        name="out",
    )(*[o for _, _, o in o_pieces], *[w for _, _, w in w_pieces], base)


def local(pixels_tokens, ln_gain, ln_bias, w_qkv, w_out):
    images, rows, _ = pixels_tokens.shape
    row_count = lax.axis_size("row")
    col_count = lax.axis_size("col")
    parts = col_count // images
    head_row = w_qkv.shape[1] // (3 * HDIM)
    heads = head_row // CHUNKS
    image = lax.axis_index("col") // parts
    dims = [1 << n for n in range(row_count.bit_length() - 1)]

    def around(value, step):
        if step % images == 0:
            return value
        return lax.ppermute(value, "col", ring(images, parts, step))

    def swaps(step, shard):
        return [(step, 0, shard)] + [
            (step, t, lax.ppermute(shard, "col", group(images, parts, t)))
            for t in range(1, parts)
        ]

    blocks = []
    for k in range(images):
        block = lax.dynamic_index_in_dim(pixels_tokens, (image + k) % images, 0, keepdims=False)
        blocks.append(around(block, k))
    normed = None
    for k in ORDER(images):
        turned = dims[k % len(dims) :] + dims[: k % len(dims)]
        pieces = spread(blocks[k], row_count, turned)
        normed = normalize(k, normed, pieces, ln_gain, ln_bias, images, parts)

    shard, early = w_qkv, []
    for step in range(images - 1):
        early += swaps(step, shard)
        if step + 2 < images:
            shard = around(shard, 1)
    acc = project_early(normed, early, parts)
    chunk_columns = heads * 3 * HDIM
    results = []
    for j in range(CHUNKS):
        last = shard[:, j * chunk_columns : (j + 1) * chunk_columns]
        last = around(last, 1)
        query, pair = project_late(j, normed, acc, swaps(images - 1, last), parts)
        pairs = [pair] + [
            lax.ppermute(pair, "col", group(images, parts, t)) for t in range(1, parts)
        ]
        outs = attend(query, pairs, images)
        outs = [around(o, -k) for k, o in enumerate(outs)]
        half = images // 2
        pieces = []
        for n in range(2):
            joined = jnp.concatenate(outs[n * half : (n + 1) * half], axis=0)
            turned = dims[n:] + dims[:n]
            pieces += [(n * half * rows, m, b) for m, b in spread(joined, row_count, turned)]
        results.append(pieces)

    shard, out_pieces = w_out, []
    for step in range(images):
        out_pieces += swaps(step, shard)
        if step + 1 < images:
            shard = around(shard, 1)
    total = pixels_tokens
    for j, pieces in enumerate(results):
        kind = jnp.float32 if j + 1 < CHUNKS else jnp.bfloat16
        total = project_out(total, pieces, out_pieces, parts, head_row, row_count, j * heads, kind)
    return total


def ORDER(images):
    return sorted(range(images), key=lambda k: (min(k, images - k), k))


def solution(mesh):
    in_specs = (P(None, "col", "row"), P(), P(), P("col", "row"), P("col", "row"))
    out_specs = P(None, "col", "row")

    def whole(pixels_tokens, *rest):
        step = jax.shard_map(
            local, mesh=mesh, in_specs=in_specs, out_specs=out_specs, check_vma=False
        )
        return step(pixels_tokens, *rest)

    return whole
```

```python
import functools
import math

import jax
import jax.numpy as jnp
from jax import lax
from jax.experimental import pallas as pl
from jax.experimental.pallas import tpu as pltpu
from jax.sharding import PartitionSpec as P

HDIM = 128
CHUNKS = 2
ANY = pl.BlockSpec(memory_space=pl.ANY)
VMEM = pl.BlockSpec(memory_space=pltpu.VMEM)


def ring(images, parts, step):
    return [
        (a * parts + b, ((a + step) % images) * parts + b)
        for a in range(images)
        for b in range(parts)
    ]


def group(images, parts, step):
    return [
        (a * parts + b, a * parts + (b + step) % parts)
        for a in range(images)
        for b in range(parts)
    ]


def tile_of(rows, limit):
    return max(t for t in range(16, limit + 1, 16) if rows % t == 0)


def cost(flops, moved, exps=0):
    return pl.CostEstimate(flops=flops, bytes_accessed=moved, transcendentals=exps)


def spread(block, rows, dims):
    pieces, n = [(0, block)], 0
    for d in dims:
        perm = [(a, a ^ d) for a in range(rows)]
        for m, b in list(pieces):
            pieces.append((m ^ d, lax.ppermute(b, "row", perm)))
            n += 1
    return pieces


def source_of(image, slot):
    table = ((0, 1, 2, 3), (1, 0, 2, 3), (2, 3, 1, 0), (3, 2, 1, 0))
    return sum(jnp.where(image == a, row[slot], 0) for a, row in enumerate(table))


def slot_of(image, source):
    return sum(jnp.where(source_of(image, slot) == source, slot, 0) for slot in range(4))


PAIRS = ((0, 1), (1, 0), (2, 3), (3, 2))
MIDDLE = ((1, 2), (2, 1))
OUTWARD = ((1, 0), (2, 3))
MIDDLES, ENDS = (1, 2), (0, 3)


def hop(parts, moves):
    return [(a * parts + p, b * parts + p) for a, b in moves for p in range(parts)]


def norm_kernel(masks, parts, gain_ref, bias_ref, *refs):
    pieces, out_ref = refs[: len(masks)], refs[-1]
    me = lax.axis_index("row")
    image = lax.axis_index("col") // parts
    width = pieces[0].shape[1]
    span = out_ref.shape[3]
    grain = min(width, span)
    total = width * len(pieces)
    floats = [ref[...].astype(jnp.float32) for ref in pieces]
    center = sum(jnp.sum(f, axis=-1, keepdims=True) for f in floats) / total
    floats = [f - center for f in floats]
    scatter = sum(jnp.sum(f * f, axis=-1, keepdims=True) for f in floats) / total
    scale = lax.rsqrt(scatter + 1e-06)
    for mask, f in zip(masks, floats):
        for part in range(width // grain):
            first = (me ^ mask) * width + part * grain
            at = pl.ds(pl.multiple_of(first, 128), grain)
            slot = slot_of(image, first // span)
            to = pl.ds(pl.multiple_of(first % span, 128), grain)
            value = f[:, part * grain : (part + 1) * grain] * scale
            out_ref[0, slot, :, to] = (value * gain_ref[:, at] + bias_ref[:, at]).astype(
                out_ref.dtype
            )


def normalize(k, held, pieces, gain, bias, images, parts):
    masks = [m for m, _ in pieces]
    rows, width = pieces[0][1].shape
    total = width * len(pieces)
    tile = tile_of(rows, 48)
    shape = (images, images, rows, total // images)
    whole = pl.BlockSpec((1, total), lambda t: (0, 0))
    extra = [] if held is None else [held]
    return pl.pallas_call(
        functools.partial(norm_kernel, masks, parts),
        grid=(rows // tile,),
        in_specs=[whole, whole]
        + [pl.BlockSpec((tile, width), lambda t: (t, 0))] * len(pieces)
        + [ANY] * len(extra),
        out_specs=pl.BlockSpec((1, images, tile, total // images), lambda t: (k, 0, t, 0)),
        out_shape=jax.ShapeDtypeStruct(shape, jnp.bfloat16),
        input_output_aliases={2 + len(pieces): 0} if extra else {},
        cost_estimate=cost(8 * rows * total, 4 * rows * total, rows),
        name="norm",
        compiler_params=pltpu.CompilerParams(vmem_limit_bytes=16 << 20),
    )(gain[None], bias[None], *[b for _, b in pieces], *extra)


def piece_copies(w_refs, tags, parts, w_v, sems, first):
    image, part = lax.axis_index("col") // parts, lax.axis_index("col") % parts
    columns = w_v.shape[1]
    waits = {}
    for ref, (slot, turn, holders) in zip(w_refs, tags):
        depth, wide = ref.shape
        at = pl.multiple_of(((part + parts - turn) % parts) * depth, 16)
        source = ref.at[:, pl.ds(first, columns)] if wide > columns else ref
        to = w_v.at[pl.ds(slot * parts * depth + at, depth)]
        copy = pltpu.make_async_copy(source, to, sems.at[slot * parts + turn])
        waits[slot, turn] = copy
        if holders is None:
            copy.start()
        else:
            held = functools.reduce(jnp.logical_or, [image == a for a in holders])
            pl.when(held)(copy.start)
    return list(waits.values())


def early_kernel(steps, parts, tags, first, x_ref, *refs):
    w_refs = refs[: len(tags)]
    out_ref, x_v, w_v, o_v, x_sem, w_sem, o_sem = refs[len(tags) :]
    images, _, _, span = x_ref.shape

    def load(k, s):
        to = x_v.at[k, :, pl.ds(s * span, span)]
        return pltpu.make_async_copy(x_ref.at[k, s], to, x_sem.at[k, s])

    def store(k):
        return pltpu.make_async_copy(o_v.at[k], out_ref.at[k], o_sem.at[k])

    copies = piece_copies(w_refs, tags, parts, w_v, w_sem, first)
    for s in range(steps):
        load(0, s).start()
    for copy in copies:
        copy.wait()

    def block(k, carry):
        for s in range(steps):
            load(k, s).wait()

        @pl.when(k + 1 < images)
        def _():
            for s in range(steps):
                load(k + 1, s).start()

        o_v[k] = jnp.dot(x_v[k], w_v[...], preferred_element_type=jnp.float32)
        store(k).start()
        return carry

    lax.fori_loop(0, images, block, 0)
    for k in range(images):
        store(k).wait()


def project_early(normed, pieces, first, columns, parts):
    images, _, rows, span = normed.shape
    tags = [(s, t, a) for s, t, a, _ in pieces]
    steps = images - 1
    tokens = images * rows
    shape = (images, rows, columns)
    return pl.pallas_call(
        functools.partial(early_kernel, steps, parts, tags, first),
        in_specs=[ANY] * (1 + len(pieces)),
        out_specs=ANY,
        out_shape=jax.ShapeDtypeStruct(shape, jnp.float32),
        scratch_shapes=[
            pltpu.VMEM((images, rows, steps * span), jnp.bfloat16),
            pltpu.VMEM((steps * span, columns), jnp.bfloat16),
            pltpu.VMEM(shape, jnp.float32),
            pltpu.SemaphoreType.DMA((images, steps)),
            pltpu.SemaphoreType.DMA((steps * parts,)),
            pltpu.SemaphoreType.DMA((images,)),
        ],
        cost_estimate=cost(2 * tokens * steps * span * columns, 2 * tokens * span * steps),
        name="early",
        compiler_params=pltpu.CompilerParams(vmem_limit_bytes=30 << 20),
    )(normed, *[w for _, _, _, w in pieces])


def late_kernel(parts, heads, tags, x_ref, acc_ref, *refs):
    w_refs = refs[: len(tags)]
    q_ref, kv_ref, x_v, a_v, w_v, x_sem, a_sem, w_sem = refs[len(tags) :]
    images, _, rows, _ = x_ref.shape
    copies = piece_copies(w_refs, [(0, t, a) for _, t, a in tags], parts, w_v, w_sem, 0)

    half = images // 2

    def loads(n):
        return [
            pltpu.make_async_copy(
                x_ref.at[n * half + k, images - 1],
                x_v.at[n, pl.ds(k * rows, rows)],
                x_sem.at[n * half + k],
            )
            for k in range(half)
        ] + [
            pltpu.make_async_copy(
                acc_ref.at[n * half + k], a_v.at[n, pl.ds(k * rows, rows)], a_sem.at[n * half + k]
            )
            for k in range(half)
        ]

    for n in range(2):
        for load in loads(n):
            load.start()
    for copy in copies:
        copy.wait()

    def block(n, carry):
        for load in loads(n):
            load.wait()
        got = a_v[n] + jnp.dot(x_v[n], w_v[...], preferred_element_type=jnp.float32)
        got = got.astype(jnp.bfloat16)
        own = pl.ds(pl.multiple_of(n * half * rows, 16), half * rows)
        for h in range(heads):
            at = 3 * HDIM * h
            q_ref[own, h * HDIM : (h + 1) * HDIM] = got[:, at : at + HDIM]
            kv_ref[own, 2 * h * HDIM : 2 * (h + 1) * HDIM] = got[:, at + HDIM : at + 3 * HDIM]
        return carry

    lax.fori_loop(0, 2, block, 0)


def project_late(normed, acc, pieces, parts):
    images, _, rows, span = normed.shape
    columns = pieces[0][3].shape[1]
    heads = columns // (3 * HDIM)
    tags = [(s, t, a) for s, t, a, _ in pieces]
    tokens = images * rows
    return pl.pallas_call(
        functools.partial(late_kernel, parts, heads, tags),
        in_specs=[ANY] * (2 + len(pieces)),
        out_specs=[VMEM, VMEM],
        out_shape=[
            jax.ShapeDtypeStruct((tokens, heads * HDIM), jnp.bfloat16),
            jax.ShapeDtypeStruct((tokens, 2 * heads * HDIM), jnp.bfloat16),
        ],
        scratch_shapes=[
            pltpu.VMEM((2, tokens // 2, span), jnp.bfloat16),
            pltpu.VMEM((2, tokens // 2, columns), jnp.float32),
            pltpu.VMEM((span, columns), jnp.bfloat16),
            pltpu.SemaphoreType.DMA((images,)),
            pltpu.SemaphoreType.DMA((images,)),
            pltpu.SemaphoreType.DMA((parts,)),
        ],
        cost_estimate=cost(2 * tokens * span * columns, 8 * tokens * columns),
        name="late",
        compiler_params=pltpu.CompilerParams(vmem_limit_bytes=24 << 20),
    )(normed, acc, *[w for _, _, _, w in pieces])


def attend_kernel(first, slots, heads, q_ref, *refs):
    kv_refs, out_refs = refs[:-slots], refs[-slots:]
    rows = out_refs[0].shape[0]
    scale = HDIM ** (-0.5) * math.log2(math.e)
    own = slice(first * rows, (first + slots) * rows)
    for h in range(heads):
        query = q_ref[own, h * HDIM : (h + 1) * HDIM]
        scores = [
            lax.dot_general(
                query,
                ref[:, 2 * h * HDIM : (2 * h + 1) * HDIM],
                (((1,), (1,)), ((), ())),
                preferred_element_type=jnp.float32,
            )
            for ref in kv_refs
        ]
        peak = functools.reduce(jnp.maximum, [jnp.max(s, axis=-1, keepdims=True) for s in scores])
        peak = peak * scale
        both = 0.0
        for s, ref in zip(scores, kv_refs):
            expo = jnp.exp2(s * scale - peak).astype(jnp.bfloat16)
            value = ref[:, (2 * h + 1) * HDIM : 2 * (h + 1) * HDIM]
            value = jnp.concatenate([value, jnp.ones_like(value)], axis=1)
            both += jnp.dot(expo, value, preferred_element_type=jnp.float32)
        got = (both[:, :HDIM] / both[:, HDIM:]).astype(jnp.bfloat16)
        for m in range(slots):
            out_refs[m][:, h * HDIM : (h + 1) * HDIM] = got[m * rows : (m + 1) * rows]


def attend(query, pairs, images, first, slots):
    tokens, wide = query.shape
    rows, heads = tokens // images, wide // HDIM
    keys = tokens * len(pairs)
    return pl.pallas_call(
        functools.partial(attend_kernel, first, slots, heads),
        in_specs=[VMEM] * (1 + len(pairs)),
        out_specs=[VMEM] * slots,
        out_shape=[jax.ShapeDtypeStruct((rows, wide), jnp.bfloat16)] * slots,
        cost_estimate=cost(
            8 * heads * slots * rows * keys * HDIM,
            4 * heads * HDIM * (tokens + keys),
            heads * slots * rows * keys,
        ),
        name="attend",
        compiler_params=pltpu.CompilerParams(vmem_limit_bytes=32 << 20),
    )(query, *pairs)


def out_kernel(parts, turns, tags, w_tags, base_ref, *refs):
    w_refs, refs = refs[: len(w_tags)], refs[len(w_tags) :]
    o_refs = refs[: len(tags)]
    out_ref, o_v, w_v, b_v, r_v, o_sem, w_sem, b_sem, r_sem = refs[len(tags) :]
    me, col = lax.axis_index("row"), lax.axis_index("col")
    images, rows, columns = base_ref.shape
    image, part = col // parts, col % parts
    half = images // 2
    spots = [(image + k) % images for k in turns]
    cuts = column_cuts(columns)
    heads = [[], []]
    for n, (chunk, mask, block) in enumerate(tags):
        size, width = o_refs[n].shape
        at = pl.multiple_of(((me ^ mask) * CHUNKS + chunk) * width, 128)
        to = o_v.at[pl.ds(block * rows, size), pl.ds(at, width)]
        heads[block // half].append(pltpu.make_async_copy(o_refs[n], to, o_sem.at[n]))
    weights = []
    for m, (begin, size) in enumerate(cuts):
        for n, (step, turn) in enumerate(w_tags):
            depth = w_refs[n].shape[0]
            place = ((image + images - step) % images) * parts + (part + parts - turn) % parts
            at = pl.multiple_of(place * depth, 16)
            span = pl.ds(begin, size)
            weights.append(
                pltpu.make_async_copy(
                    w_refs[n].at[:, span], w_v.at[pl.ds(at, depth), span], w_sem.at[m, n]
                )
            )
    bases = [
        pltpu.make_async_copy(base_ref.at[spot], b_v.at[n], b_sem.at[n])
        for n, spot in enumerate(spots)
    ]
    per = len(w_tags)
    for copy in heads[0] + weights[:per] + heads[1] + bases + weights[per:]:
        copy.start()
    for copy in heads[0] + heads[1]:
        copy.wait()

    def store(m, n, spot):
        span = pl.ds(*cuts[m])
        return pltpu.make_async_copy(
            r_v.at[n, :, span], out_ref.at[spot, :, span], r_sem.at[m, n]
        )

    for m, (begin, size) in enumerate(cuts):
        for copy in weights[m * per : (m + 1) * per]:
            copy.wait()
        if m == 0:
            for copy in bases:
                copy.wait()

        def body(block, carry, m=m, begin=begin, size=size):
            at = pl.ds(pl.multiple_of(block * half * rows, 16), half * rows)
            got = jnp.dot(
                o_v[at, :], w_v[:, begin : begin + size], preferred_element_type=jnp.float32
            )
            for k in range(half):
                n = block * half + k
                mine = got[k * rows : (k + 1) * rows]
                r_v[n, :, begin : begin + size] = (
                    b_v[n, :, begin : begin + size].astype(jnp.float32) + mine
                ).astype(r_v.dtype)
                store(m, n, jnp.where(block == 0, spots[k], spots[half + k])).start()
            return carry

        lax.fori_loop(0, 2, body, 0)
    for m in range(len(cuts)):
        for n, spot in enumerate(spots):
            store(m, n, spot).wait()


def column_cuts(columns):
    first = -(-columns // 512) * 256
    return ((0, first), (first, columns - first))


def project_out(base, w_pieces, pieces, parts, row_count, turns):
    tags = [(chunk, m, block) for chunk, m, block, _ in pieces]
    w_tags = [(s, t) for s, t, _ in w_pieces]
    images, rows, columns = base.shape
    width = pieces[0][3].shape[1]
    deep = len(w_pieces) * w_pieces[0][2].shape[0]
    cuts = len(column_cuts(columns))
    return pl.pallas_call(
        functools.partial(out_kernel, parts, turns, tags, w_tags),
        in_specs=[ANY] * (1 + len(w_tags) + len(tags)),
        out_specs=ANY,
        out_shape=jax.ShapeDtypeStruct(base.shape, jnp.bfloat16),
        scratch_shapes=[
            pltpu.VMEM((images * rows, row_count * CHUNKS * width), jnp.bfloat16),
            pltpu.VMEM((deep, columns), jnp.bfloat16),
            pltpu.VMEM(base.shape, base.dtype),
            pltpu.VMEM(base.shape, jnp.bfloat16),
            pltpu.SemaphoreType.DMA((len(tags),)),
            pltpu.SemaphoreType.DMA((cuts, len(w_tags))),
            pltpu.SemaphoreType.DMA((images,)),
            pltpu.SemaphoreType.DMA((cuts, images)),
        ],
        cost_estimate=cost(2 * images * rows * columns * deep, 8 * images * rows * columns),
        name="out",
        compiler_params=pltpu.CompilerParams(vmem_limit_bytes=30 << 20),
    )(base, *[w for _, _, w in w_pieces], *[o for _, _, _, o in pieces])


def local(pixels_tokens, ln_gain, ln_bias, w_qkv, w_out):
    images, _, _ = pixels_tokens.shape
    row_count = lax.axis_size("row")
    col_count = lax.axis_size("col")
    parts = col_count // images
    head_row = w_qkv.shape[1] // (3 * HDIM)
    heads = head_row // CHUNKS
    image = lax.axis_index("col") // parts
    dims = [1 << n for n in range(row_count.bit_length() - 1)]

    def around(value, step):
        if step % images == 0:
            return value
        return lax.ppermute(value, "col", ring(images, parts, step))

    def swaps(step, shard):
        return [(step, 0, shard)] + [
            (step, t, lax.ppermute(shard, "col", group(images, parts, t)))
            for t in range(1, parts)
        ]

    shifts = SLOTS(images)
    blocks = []
    for k in shifts:
        block = lax.dynamic_index_in_dim(pixels_tokens, (image + k) % images, 0, keepdims=False)
        blocks.append(around(block, k))
    normed = None
    for slot in NORMS(images):
        k = shifts[slot]
        turned = dims[k % len(dims) :] + dims[: k % len(dims)]
        pieces = spread(blocks[slot], row_count, turned)
        normed = normalize(slot, normed, pieces, ln_gain, ln_bias, images, parts)

    columns = heads * 3 * HDIM
    own = [(0, t, None, w) for _, t, w in swaps(0, w_qkv)]

    def arrive(slot, holders, value, moves):
        got = lax.ppermute(value, "col", hop(parts, moves))
        there = [(a, a) for a in (holders or range(images))]
        turned = [(slot, 0, holders, got)]
        for t in range(1, parts):
            perm = [
                (a * parts + p, a * parts + (p + t) % parts) for a, _ in there for p in range(parts)
            ]
            turned.append((slot, t, holders, lax.ppermute(got, "col", perm)))
        return got, turned

    results = []
    for j in range(CHUNKS):
        shard = w_qkv[:, j * columns : (j + 1) * columns]
        near, one = arrive(1, None, shard, PAIRS)
        across, two = arrive(2, MIDDLES, shard, MIDDLE)
        _, three = arrive(2, ENDS, across, OUTWARD)
        far, four = arrive(3, MIDDLES, near, MIDDLE)
        _, five = arrive(3, ENDS, far, OUTWARD)
        first = own + one + two + three
        acc = project_early(normed, first, j * columns, columns, parts)
        query, pair = project_late(normed, acc, four + five, parts)
        pairs = [pair] + [
            lax.ppermute(pair, "col", group(images, parts, t)) for t in range(1, parts)
        ]
        half = images // 2
        outs = []
        for n in range(2):
            mine = shifts[n * half : (n + 1) * half]
            got = attend(query, pairs, images, n * half, half)
            outs += [around(o, -k) for k, o in zip(mine, got)]
        if j + 1 < CHUNKS:
            pieces = []
            for n in range(2):
                joined = jnp.concatenate(outs[n * half : (n + 1) * half], axis=0)
                turned = dims[n:] + dims[:n]
                pieces += [(n * half, spread(joined, row_count, turned))]
            results.append(pieces)
            continue
        pieces = []
        for n, (k, o) in enumerate(zip(shifts, outs)):
            turned = dims[n % len(dims) :] + dims[: n % len(dims)]
            pieces.append((n, spread(o, row_count, turned)))
        results.append(pieces)

    shard, out_pieces = w_out, []
    for step in range(images):
        out_pieces += swaps(step, shard)
        if step + 1 < images:
            shard = around(shard, 1)
    pieces = [
        (j, m, n, o) for j in range(CHUNKS) for n, got in results[j] for m, o in got
    ]
    return project_out(pixels_tokens, out_pieces, pieces, parts, row_count, shifts)


def SLOTS(images):
    return sorted(range(1, images), key=lambda k: (min(k, images - k), k)) + [0]


def NORMS(images):
    return [images - 1, 0] + list(range(images - 2, 0, -1))


def solution(mesh):
    in_specs = (P(None, "col", "row"), P(), P(), P("col", "row"), P("col", "row"))
    out_specs = P(None, "col", "row")

    def whole(pixels_tokens, *rest):
        step = jax.shard_map(
            local, mesh=mesh, in_specs=in_specs, out_specs=out_specs, check_vma=False
        )
        return step(pixels_tokens, *rest)

    return whole
```

```python
import functools
import math

import jax
import jax.numpy as jnp
from jax import lax
from jax.experimental import pallas as pl
from jax.experimental.pallas import tpu as pltpu
from jax.sharding import PartitionSpec as P

HDIM = 128
CHUNKS = 2
ANY = pl.BlockSpec(memory_space=pl.ANY)
VMEM = pl.BlockSpec(memory_space=pltpu.VMEM)


def ring(images, parts, step):
    return [
        (a * parts + b, ((a + step) % images) * parts + b)
        for a in range(images)
        for b in range(parts)
    ]


def group(images, parts, step):
    return [
        (a * parts + b, a * parts + (b + step) % parts)
        for a in range(images)
        for b in range(parts)
    ]


def tile_of(rows, limit):
    return max(t for t in range(16, limit + 1, 16) if rows % t == 0)


def cost(flops, moved, exps=0):
    return pl.CostEstimate(flops=flops, bytes_accessed=moved, transcendentals=exps)


def spread(block, rows, dims):
    pieces, n = [(0, block)], 0
    for d in dims:
        perm = [(a, a ^ d) for a in range(rows)]
        for m, b in list(pieces):
            pieces.append((m ^ d, lax.ppermute(b, "row", perm)))
            n += 1
    return pieces


def source_of(image, slot):
    table = ((0, 1, 2, 3), (1, 0, 2, 3), (2, 3, 1, 0), (3, 2, 1, 0))
    return sum(jnp.where(image == a, row[slot], 0) for a, row in enumerate(table))


def slot_of(image, source):
    return sum(jnp.where(source_of(image, slot) == source, slot, 0) for slot in range(4))


PAIRS = ((0, 1), (1, 0), (2, 3), (3, 2))
MIDDLE = ((1, 2), (2, 1))
OUTWARD = ((1, 0), (2, 3))
MIDDLES, ENDS = (1, 2), (0, 3)


def hop(parts, moves):
    return [(a * parts + p, b * parts + p) for a, b in moves for p in range(parts)]


def norm_kernel(masks, parts, gain_ref, bias_ref, *refs):
    pieces, out_ref = refs[: len(masks)], refs[-1]
    me = lax.axis_index("row")
    image = lax.axis_index("col") // parts
    width = pieces[0].shape[1]
    span = out_ref.shape[3]
    grain = min(width, span)
    total = width * len(pieces)
    floats = [ref[...].astype(jnp.float32) for ref in pieces]
    center = sum(jnp.sum(f, axis=-1, keepdims=True) for f in floats) / total
    floats = [f - center for f in floats]
    scatter = sum(jnp.sum(f * f, axis=-1, keepdims=True) for f in floats) / total
    scale = lax.rsqrt(scatter + 1e-06)
    for mask, f in zip(masks, floats):
        for part in range(width // grain):
            first = (me ^ mask) * width + part * grain
            at = pl.ds(pl.multiple_of(first, 128), grain)
            slot = slot_of(image, first // span)
            to = pl.ds(pl.multiple_of(first % span, 128), grain)
            value = f[:, part * grain : (part + 1) * grain] * scale
            out_ref[0, slot, :, to] = (value * gain_ref[:, at] + bias_ref[:, at]).astype(
                out_ref.dtype
            )


def normalize(k, held, pieces, gain, bias, images, parts):
    masks = [m for m, _ in pieces]
    rows, width = pieces[0][1].shape
    total = width * len(pieces)
    tile = tile_of(rows, 48)
    shape = (images, images, rows, total // images)
    whole = pl.BlockSpec((1, total), lambda t: (0, 0))
    extra = [] if held is None else [held]
    return pl.pallas_call(
        functools.partial(norm_kernel, masks, parts),
        grid=(rows // tile,),
        in_specs=[whole, whole]
        + [pl.BlockSpec((tile, width), lambda t: (t, 0))] * len(pieces)
        + [ANY] * len(extra),
        out_specs=pl.BlockSpec((1, images, tile, total // images), lambda t: (k, 0, t, 0)),
        out_shape=jax.ShapeDtypeStruct(shape, jnp.bfloat16),
        input_output_aliases={2 + len(pieces): 0} if extra else {},
        cost_estimate=cost(8 * rows * total, 4 * rows * total, rows),
        name="norm",
        compiler_params=pltpu.CompilerParams(vmem_limit_bytes=16 << 20),
    )(gain[None], bias[None], *[b for _, b in pieces], *extra)


def piece_copies(w_refs, tags, parts, w_v, sems, first):
    image, part = lax.axis_index("col") // parts, lax.axis_index("col") % parts
    columns = w_v.shape[1]
    waits = {}
    for ref, (slot, turn, holders) in zip(w_refs, tags):
        depth, wide = ref.shape
        at = pl.multiple_of(((part + parts - turn) % parts) * depth, 16)
        source = ref.at[:, pl.ds(first, columns)] if wide > columns else ref
        to = w_v.at[pl.ds(slot * parts * depth + at, depth)]
        copy = pltpu.make_async_copy(source, to, sems.at[slot * parts + turn])
        waits[slot, turn] = copy
        if holders is None:
            copy.start()
        else:
            held = functools.reduce(jnp.logical_or, [image == a for a in holders])
            pl.when(held)(copy.start)
    return list(waits.values())


def early_kernel(steps, parts, tags, first, x_ref, *refs):
    w_refs = refs[: len(tags)]
    out_ref, x_v, w_v, o_v, x_sem, w_sem, o_sem = refs[len(tags) :]
    images, _, _, span = x_ref.shape

    def load(k, s):
        to = x_v.at[k, :, pl.ds(s * span, span)]
        return pltpu.make_async_copy(x_ref.at[k, s], to, x_sem.at[k, s])

    def store(k):
        return pltpu.make_async_copy(o_v.at[k], out_ref.at[k], o_sem.at[k])

    copies = piece_copies(w_refs, tags, parts, w_v, w_sem, first)
    for s in range(steps):
        load(0, s).start()
    for copy in copies:
        copy.wait()

    def block(k, carry):
        for s in range(steps):
            load(k, s).wait()

        @pl.when(k + 1 < images)
        def _():
            for s in range(steps):
                load(k + 1, s).start()

        o_v[k] = jnp.dot(x_v[k], w_v[...], preferred_element_type=jnp.float32)
        store(k).start()
        return carry

    lax.fori_loop(0, images, block, 0)
    for k in range(images):
        store(k).wait()


def project_early(normed, pieces, first, columns, parts):
    images, _, rows, span = normed.shape
    tags = [(s, t, a) for s, t, a, _ in pieces]
    steps = images - 1
    tokens = images * rows
    shape = (images, rows, columns)
    return pl.pallas_call(
        functools.partial(early_kernel, steps, parts, tags, first),
        in_specs=[ANY] * (1 + len(pieces)),
        out_specs=ANY,
        out_shape=jax.ShapeDtypeStruct(shape, jnp.float32),
        scratch_shapes=[
            pltpu.VMEM((images, rows, steps * span), jnp.bfloat16),
            pltpu.VMEM((steps * span, columns), jnp.bfloat16),
            pltpu.VMEM(shape, jnp.float32),
            pltpu.SemaphoreType.DMA((images, steps)),
            pltpu.SemaphoreType.DMA((steps * parts,)),
            pltpu.SemaphoreType.DMA((images,)),
        ],
        cost_estimate=cost(2 * tokens * steps * span * columns, 2 * tokens * span * steps),
        name="early",
        compiler_params=pltpu.CompilerParams(vmem_limit_bytes=30 << 20),
    )(normed, *[w for _, _, _, w in pieces])


def late_kernel(parts, heads, tags, x_ref, acc_ref, *refs):
    w_refs = refs[: len(tags)]
    q_ref, kv_ref, x_v, a_v, w_v, x_sem, a_sem, w_sem = refs[len(tags) :]
    images, _, rows, _ = x_ref.shape
    copies = piece_copies(w_refs, [(0, t, a) for _, t, a in tags], parts, w_v, w_sem, 0)

    half = images // 2

    def loads(n):
        return [
            pltpu.make_async_copy(
                x_ref.at[n * half + k, images - 1],
                x_v.at[n, pl.ds(k * rows, rows)],
                x_sem.at[n * half + k],
            )
            for k in range(half)
        ] + [
            pltpu.make_async_copy(
                acc_ref.at[n * half + k], a_v.at[n, pl.ds(k * rows, rows)], a_sem.at[n * half + k]
            )
            for k in range(half)
        ]

    for n in range(2):
        for load in loads(n):
            load.start()
    for copy in copies:
        copy.wait()

    def block(n, carry):
        for load in loads(n):
            load.wait()
        got = a_v[n] + jnp.dot(x_v[n], w_v[...], preferred_element_type=jnp.float32)
        got = got.astype(jnp.bfloat16)
        own = pl.ds(pl.multiple_of(n * half * rows, 16), half * rows)
        for h in range(heads):
            at = 3 * HDIM * h
            q_ref[own, h * HDIM : (h + 1) * HDIM] = got[:, at : at + HDIM]
            kv_ref[own, 2 * h * HDIM : 2 * (h + 1) * HDIM] = got[:, at + HDIM : at + 3 * HDIM]
        return carry

    lax.fori_loop(0, 2, block, 0)


def project_late(normed, acc, pieces, parts):
    images, _, rows, span = normed.shape
    columns = pieces[0][3].shape[1]
    heads = columns // (3 * HDIM)
    tags = [(s, t, a) for s, t, a, _ in pieces]
    tokens = images * rows
    return pl.pallas_call(
        functools.partial(late_kernel, parts, heads, tags),
        in_specs=[ANY] * (2 + len(pieces)),
        out_specs=[VMEM, VMEM],
        out_shape=[
            jax.ShapeDtypeStruct((tokens, heads * HDIM), jnp.bfloat16),
            jax.ShapeDtypeStruct((tokens, 2 * heads * HDIM), jnp.bfloat16),
        ],
        scratch_shapes=[
            pltpu.VMEM((2, tokens // 2, span), jnp.bfloat16),
            pltpu.VMEM((2, tokens // 2, columns), jnp.float32),
            pltpu.VMEM((span, columns), jnp.bfloat16),
            pltpu.SemaphoreType.DMA((images,)),
            pltpu.SemaphoreType.DMA((images,)),
            pltpu.SemaphoreType.DMA((parts,)),
        ],
        cost_estimate=cost(2 * tokens * span * columns, 8 * tokens * columns),
        name="late",
        compiler_params=pltpu.CompilerParams(vmem_limit_bytes=24 << 20),
    )(normed, acc, *[w for _, _, _, w in pieces])


def attend_kernel(first, slots, heads, q_ref, *refs):
    kv_refs, out_refs = refs[:-slots], refs[-slots:]
    rows = out_refs[0].shape[0]
    scale = HDIM ** (-0.5) * math.log2(math.e)
    own = slice(first * rows, (first + slots) * rows)
    for h in range(heads):
        query = q_ref[own, h * HDIM : (h + 1) * HDIM]
        scores = [
            lax.dot_general(
                query,
                ref[:, 2 * h * HDIM : (2 * h + 1) * HDIM],
                (((1,), (1,)), ((), ())),
                preferred_element_type=jnp.float32,
            )
            for ref in kv_refs
        ]
        peak = functools.reduce(jnp.maximum, [jnp.max(s, axis=-1, keepdims=True) for s in scores])
        peak = peak * scale
        both = 0.0
        for s, ref in zip(scores, kv_refs):
            expo = jnp.exp2(s * scale - peak).astype(jnp.bfloat16)
            value = ref[:, (2 * h + 1) * HDIM : 2 * (h + 1) * HDIM]
            value = jnp.concatenate([value, jnp.ones_like(value)], axis=1)
            both += jnp.dot(expo, value, preferred_element_type=jnp.float32)
        got = (both[:, :HDIM] / both[:, HDIM:]).astype(jnp.bfloat16)
        for m in range(slots):
            out_refs[m][:, h * HDIM : (h + 1) * HDIM] = got[m * rows : (m + 1) * rows]


def attend(query, pairs, images, first, slots):
    tokens, wide = query.shape
    rows, heads = tokens // images, wide // HDIM
    keys = tokens * len(pairs)
    return pl.pallas_call(
        functools.partial(attend_kernel, first, slots, heads),
        in_specs=[VMEM] * (1 + len(pairs)),
        out_specs=[VMEM] * slots,
        out_shape=[jax.ShapeDtypeStruct((rows, wide), jnp.bfloat16)] * slots,
        cost_estimate=cost(
            8 * heads * slots * rows * keys * HDIM,
            4 * heads * HDIM * (tokens + keys),
            heads * slots * rows * keys,
        ),
        name="attend",
        compiler_params=pltpu.CompilerParams(vmem_limit_bytes=32 << 20),
    )(query, *pairs)


def out_kernel(parts, turns, tags, w_tags, last, base_ref, *refs):
    w_refs, refs = refs[: len(w_tags)], refs[len(w_tags) :]
    o_refs = refs[: len(tags)]
    outs = refs[len(tags) : len(tags) + (1 if last else 2)]
    o_v, w_v, b_v, r_v, o_sem, w_sem, b_sem, r_sem, k_sem = refs[len(tags) + len(outs) :]
    me, col = lax.axis_index("row"), lax.axis_index("col")
    images, rows, columns = base_ref.shape
    image, part = col // parts, col % parts
    half = images // 2
    deep = w_v.shape[0]
    spots = [(image + k) % images for k in turns]
    cuts = column_cuts(columns)
    heads = []
    for n, (chunk, mask, block) in enumerate(tags):
        if last:
            heads.append(pltpu.make_async_copy(o_refs[n], o_v, o_sem.at[n]))
            continue
        size, width = o_refs[n].shape
        per = parts * w_refs[0].shape[0] // (CHUNKS * width)
        other = me ^ mask
        slot = (image + images - other // per) % images
        at = pl.multiple_of(((slot * per + other % per) * CHUNKS + chunk) * width, 128)
        to = o_v.at[pl.ds(block * rows, size), pl.ds(at, width)]
        heads.append(pltpu.make_async_copy(o_refs[n], to, o_sem.at[n]))
    weights = []
    for m, (begin, size) in enumerate(cuts):
        for n, (step, turn) in enumerate(w_tags):
            depth = w_refs[n].shape[0]
            first = 0 if last else step * parts * depth
            at = pl.multiple_of(first + (part + parts - turn) % parts * depth, 16)
            span = pl.ds(begin, size)
            weights.append(
                pltpu.make_async_copy(
                    w_refs[n].at[:, span], w_v.at[pl.ds(at, depth), span], w_sem.at[m, n]
                )
            )
    bases = [
        pltpu.make_async_copy(base_ref.at[n if last else spot], b_v.at[n], b_sem.at[n])
        for n, spot in enumerate(spots)
    ]
    per = len(w_tags)
    for copy in heads + weights[:per] + bases + weights[per:]:
        copy.start()
    for copy in heads:
        copy.wait()
    keep = None
    if not last:
        keep = pltpu.make_async_copy(
            o_v.at[:, pl.ds(deep, o_v.shape[1] - deep)], outs[1], k_sem.at[0]
        )
        keep.start()

    def store(m, n, spot):
        span = pl.ds(*cuts[m])
        to = spot if last else n
        return pltpu.make_async_copy(r_v.at[n, :, span], outs[0].at[to, :, span], r_sem.at[m, n])

    for m, (begin, size) in enumerate(cuts):
        for copy in weights[m * per : (m + 1) * per]:
            copy.wait()
        if m == 0:
            for copy in bases:
                copy.wait()

        def body(block, carry, m=m, begin=begin, size=size):
            at = pl.ds(pl.multiple_of(block * half * rows, 16), half * rows)
            got = jnp.dot(
                o_v[at, :deep], w_v[:, begin : begin + size], preferred_element_type=jnp.float32
            )
            for k in range(half):
                n = block * half + k
                mine = got[k * rows : (k + 1) * rows]
                r_v[n, :, begin : begin + size] = (
                    b_v[n, :, begin : begin + size].astype(jnp.float32) + mine
                ).astype(r_v.dtype)
                store(m, n, jnp.where(block == 0, spots[k], spots[half + k])).start()
            return carry

        lax.fori_loop(0, 2, body, 0)
    for m in range(len(cuts)):
        for n, spot in enumerate(spots):
            store(m, n, spot).wait()
    if keep is not None:
        keep.wait()


def column_cuts(columns):
    first = -(-columns // 512) * 256
    return ((0, first), (first, columns - first))


def project_out(base, w_pieces, pieces, parts, turns, last):
    tags = [(chunk, m, block) for chunk, m, block, _ in pieces]
    w_tags = [(s, t) for s, t, _ in w_pieces]
    images, rows, columns = base.shape
    depth = w_pieces[0][2].shape[0]
    deep = len(w_pieces) * depth
    wide = deep if last else deep + parts * depth
    cuts = len(column_cuts(columns))
    kind = jnp.bfloat16 if last else jnp.float32
    tokens = images * rows
    shapes = [jax.ShapeDtypeStruct(base.shape, kind)]
    if not last:
        shapes.append(jax.ShapeDtypeStruct((tokens, wide - deep), jnp.bfloat16))
    return pl.pallas_call(
        functools.partial(out_kernel, parts, turns, tags, w_tags, last),
        in_specs=[ANY] * (1 + len(w_tags) + len(tags)),
        out_specs=[ANY] * len(shapes),
        out_shape=shapes,
        scratch_shapes=[
            pltpu.VMEM((tokens, wide), jnp.bfloat16),
            pltpu.VMEM((deep, columns), jnp.bfloat16),
            pltpu.VMEM(base.shape, base.dtype),
            pltpu.VMEM(base.shape, kind),
            pltpu.SemaphoreType.DMA((len(tags),)),
            pltpu.SemaphoreType.DMA((cuts, len(w_tags))),
            pltpu.SemaphoreType.DMA((images,)),
            pltpu.SemaphoreType.DMA((cuts, images)),
            pltpu.SemaphoreType.DMA((1,)),
        ],
        cost_estimate=cost(2 * tokens * columns * deep, 8 * tokens * columns),
        name="out",
        compiler_params=pltpu.CompilerParams(vmem_limit_bytes=28 << 20),
    )(base, *[w for _, _, w in w_pieces], *[o for _, _, _, o in pieces])


def local(pixels_tokens, ln_gain, ln_bias, w_qkv, w_out):
    images, _, _ = pixels_tokens.shape
    row_count = lax.axis_size("row")
    col_count = lax.axis_size("col")
    parts = col_count // images
    head_row = w_qkv.shape[1] // (3 * HDIM)
    heads = head_row // CHUNKS
    image = lax.axis_index("col") // parts
    dims = [1 << n for n in range(row_count.bit_length() - 1)]

    def around(value, step):
        if step % images == 0:
            return value
        return lax.ppermute(value, "col", ring(images, parts, step))

    def swaps(step, shard):
        return [(step, 0, shard)] + [
            (step, t, lax.ppermute(shard, "col", group(images, parts, t)))
            for t in range(1, parts)
        ]

    shifts = SLOTS(images)
    blocks = []
    for k in shifts:
        block = lax.dynamic_index_in_dim(pixels_tokens, (image + k) % images, 0, keepdims=False)
        blocks.append(around(block, k))
    normed = None
    for slot in NORMS(images):
        k = shifts[slot]
        turned = dims[k % len(dims) :] + dims[: k % len(dims)]
        pieces = spread(blocks[slot], row_count, turned)
        normed = normalize(slot, normed, pieces, ln_gain, ln_bias, images, parts)

    columns = heads * 3 * HDIM
    own = [(0, t, None, w) for _, t, w in swaps(0, w_qkv)]

    def arrive(slot, holders, value, moves):
        got = lax.ppermute(value, "col", hop(parts, moves))
        there = [(a, a) for a in (holders or range(images))]
        turned = [(slot, 0, holders, got)]
        for t in range(1, parts):
            perm = [
                (a * parts + p, a * parts + (p + t) % parts) for a, _ in there for p in range(parts)
            ]
            turned.append((slot, t, holders, lax.ppermute(got, "col", perm)))
        return got, turned

    results = []
    for j in range(CHUNKS):
        shard = w_qkv[:, j * columns : (j + 1) * columns]
        near, one = arrive(1, None, shard, PAIRS)
        across, two = arrive(2, MIDDLES, shard, MIDDLE)
        _, three = arrive(2, ENDS, across, OUTWARD)
        far, four = arrive(3, MIDDLES, near, MIDDLE)
        _, five = arrive(3, ENDS, far, OUTWARD)
        first = own + one + two + three
        acc = project_early(normed, first, j * columns, columns, parts)
        query, pair = project_late(normed, acc, four + five, parts)
        pairs = [pair] + [
            lax.ppermute(pair, "col", group(images, parts, t)) for t in range(1, parts)
        ]
        half = images // 2
        outs = []
        for n in range(2):
            mine = shifts[n * half : (n + 1) * half]
            got = attend(query, pairs, images, n * half, half)
            outs += [around(o, -k) for k, o in zip(mine, got)]
        if j + 1 < CHUNKS:
            pieces = []
            for n in range(2):
                joined = jnp.concatenate(outs[n * half : (n + 1) * half], axis=0)
                turned = dims[n:] + dims[:n]
                pieces += [(n * half, spread(joined, row_count, turned))]
            results.append(pieces)
            continue
        pieces = []
        for n, (k, o) in enumerate(zip(shifts, outs)):
            turned = dims[n % len(dims) :] + dims[: n % len(dims)]
            pieces.append((n, spread(o, row_count, turned)))
        results.append(pieces)

    shard, out_pieces = w_out, []
    for step in range(images):
        out_pieces += swaps(step, shard)
        if step + 1 < images:
            shard = around(shard, 1)
    pieces = [
        (j, m, n, o) for j in range(CHUNKS) for n, got in results[j] for m, o in got
    ]
    split = len(out_pieces) - parts
    total, rest = project_out(pixels_tokens, out_pieces[:split], pieces, parts, shifts, False)
    pieces = [(0, 0, 0, rest)]
    return project_out(total, out_pieces[split:], pieces, parts, shifts, True)[0]


def SLOTS(images):
    return sorted(range(1, images), key=lambda k: (min(k, images - k), k)) + [0]


def NORMS(images):
    return [images - 1, 0] + list(range(images - 2, 0, -1))


def solution(mesh):
    in_specs = (P(None, "col", "row"), P(), P(), P("col", "row"), P("col", "row"))
    out_specs = P(None, "col", "row")

    def whole(pixels_tokens, *rest):
        step = jax.shard_map(
            local, mesh=mesh, in_specs=in_specs, out_specs=out_specs, check_vma=False
        )
        return step(pixels_tokens, *rest)

    return whole
```

```python
import functools
import math

import jax
import jax.numpy as jnp
from jax import lax
from jax.experimental import pallas as pl
from jax.experimental.pallas import tpu as pltpu
from jax.sharding import PartitionSpec as P

HDIM = 128
CHUNKS = 2
ANY = pl.BlockSpec(memory_space=pl.ANY)
VMEM = pl.BlockSpec(memory_space=pltpu.VMEM)


def ring(images, parts, step):
    return [
        (a * parts + b, ((a + step) % images) * parts + b)
        for a in range(images)
        for b in range(parts)
    ]


def group(images, parts, step):
    return [
        (a * parts + b, a * parts + (b + step) % parts)
        for a in range(images)
        for b in range(parts)
    ]


def tile_of(rows, limit):
    return max(t for t in range(16, limit + 1, 16) if rows % t == 0)


def cost(flops, moved, exps=0):
    return pl.CostEstimate(flops=flops, bytes_accessed=moved, transcendentals=exps)


def spread(block, rows, dims):
    pieces, n = [(0, block)], 0
    for d in dims:
        perm = [(a, a ^ d) for a in range(rows)]
        for m, b in list(pieces):
            pieces.append((m ^ d, lax.ppermute(b, "row", perm)))
            n += 1
    return pieces


def source_of(image, slot):
    table = ((0, 1, 2, 3), (1, 0, 2, 3), (2, 3, 1, 0), (3, 2, 1, 0))
    return sum(jnp.where(image == a, row[slot], 0) for a, row in enumerate(table))


def slot_of(image, source):
    return sum(jnp.where(source_of(image, slot) == source, slot, 0) for slot in range(4))


PAIRS = ((0, 1), (1, 0), (2, 3), (3, 2))
MIDDLE = ((1, 2), (2, 1))
OUTWARD = ((1, 0), (2, 3))
MIDDLES, ENDS = (1, 2), (0, 3)


def hop(parts, moves):
    return [(a * parts + p, b * parts + p) for a, b in moves for p in range(parts)]


def norm_kernel(masks, parts, gain_ref, bias_ref, *refs):
    pieces, out_ref = refs[: len(masks)], refs[-1]
    me = lax.axis_index("row")
    image = lax.axis_index("col") // parts
    width = pieces[0].shape[1]
    span = out_ref.shape[3]
    grain = min(width, span)
    total = width * len(pieces)
    floats = [ref[...].astype(jnp.float32) for ref in pieces]
    center = sum(jnp.sum(f, axis=-1, keepdims=True) for f in floats) / total
    floats = [f - center for f in floats]
    scatter = sum(jnp.sum(f * f, axis=-1, keepdims=True) for f in floats) / total
    scale = lax.rsqrt(scatter + 1e-06)
    for mask, f in zip(masks, floats):
        for part in range(width // grain):
            first = (me ^ mask) * width + part * grain
            at = pl.ds(pl.multiple_of(first, 128), grain)
            slot = slot_of(image, first // span)
            to = pl.ds(pl.multiple_of(first % span, 128), grain)
            value = f[:, part * grain : (part + 1) * grain] * scale
            out_ref[0, slot, :, to] = (value * gain_ref[:, at] + bias_ref[:, at]).astype(
                out_ref.dtype
            )


def normalize(k, held, pieces, gain, bias, images, parts):
    masks = [m for m, _ in pieces]
    rows, width = pieces[0][1].shape
    total = width * len(pieces)
    tile = tile_of(rows, 48)
    shape = (images, images, rows, total // images)
    whole = pl.BlockSpec((1, total), lambda t: (0, 0))
    extra = [] if held is None else [held]
    return pl.pallas_call(
        functools.partial(norm_kernel, masks, parts),
        grid=(rows // tile,),
        in_specs=[whole, whole]
        + [pl.BlockSpec((tile, width), lambda t: (t, 0))] * len(pieces)
        + [ANY] * len(extra),
        out_specs=pl.BlockSpec((1, images, tile, total // images), lambda t: (k, 0, t, 0)),
        out_shape=jax.ShapeDtypeStruct(shape, jnp.bfloat16),
        input_output_aliases={2 + len(pieces): 0} if extra else {},
        cost_estimate=cost(8 * rows * total, 4 * rows * total, rows),
        name="norm",
        compiler_params=pltpu.CompilerParams(vmem_limit_bytes=16 << 20),
    )(gain[None], bias[None], *[b for _, b in pieces], *extra)


def piece_copies(w_refs, tags, parts, w_v, sems, first):
    image, part = lax.axis_index("col") // parts, lax.axis_index("col") % parts
    columns = w_v.shape[1]
    waits = {}
    for ref, (slot, turn, holders) in zip(w_refs, tags):
        depth, wide = ref.shape
        at = pl.multiple_of(((part + parts - turn) % parts) * depth, 16)
        source = ref.at[:, pl.ds(first, columns)] if wide > columns else ref
        to = w_v.at[pl.ds(slot * parts * depth + at, depth)]
        copy = pltpu.make_async_copy(source, to, sems.at[slot * parts + turn])
        waits[slot, turn] = copy
        if holders is None:
            copy.start()
        else:
            held = functools.reduce(jnp.logical_or, [image == a for a in holders])
            pl.when(held)(copy.start)
    return list(waits.values())


def early_kernel(steps, parts, tags, first, x_ref, *refs):
    w_refs = refs[: len(tags)]
    out_ref, x_v, w_v, o_v, x_sem, w_sem, o_sem = refs[len(tags) :]
    images, _, _, span = x_ref.shape

    def load(k, s):
        to = x_v.at[k, :, pl.ds(s * span, span)]
        return pltpu.make_async_copy(x_ref.at[k, s], to, x_sem.at[k, s])

    def store(k):
        return pltpu.make_async_copy(o_v.at[k], out_ref.at[k], o_sem.at[k])

    copies = piece_copies(w_refs, tags, parts, w_v, w_sem, first)
    for s in range(steps):
        load(0, s).start()
    for copy in copies:
        copy.wait()

    def block(k, carry):
        for s in range(steps):
            load(k, s).wait()

        @pl.when(k + 1 < images)
        def _():
            for s in range(steps):
                load(k + 1, s).start()

        o_v[k] = jnp.dot(x_v[k], w_v[...], preferred_element_type=jnp.float32)
        store(k).start()
        return carry

    lax.fori_loop(0, images, block, 0)
    for k in range(images):
        store(k).wait()


def project_early(normed, pieces, first, columns, parts):
    images, _, rows, span = normed.shape
    tags = [(s, t, a) for s, t, a, _ in pieces]
    steps = images - 1
    tokens = images * rows
    shape = (images, rows, columns)
    return pl.pallas_call(
        functools.partial(early_kernel, steps, parts, tags, first),
        in_specs=[ANY] * (1 + len(pieces)),
        out_specs=ANY,
        out_shape=jax.ShapeDtypeStruct(shape, jnp.float32),
        scratch_shapes=[
            pltpu.VMEM((images, rows, steps * span), jnp.bfloat16),
            pltpu.VMEM((steps * span, columns), jnp.bfloat16),
            pltpu.VMEM(shape, jnp.float32),
            pltpu.SemaphoreType.DMA((images, steps)),
            pltpu.SemaphoreType.DMA((steps * parts,)),
            pltpu.SemaphoreType.DMA((images,)),
        ],
        cost_estimate=cost(2 * tokens * steps * span * columns, 2 * tokens * span * steps),
        name="early",
        compiler_params=pltpu.CompilerParams(vmem_limit_bytes=30 << 20),
    )(normed, *[w for _, _, _, w in pieces])


def late_kernel(parts, heads, tags, x_ref, acc_ref, *refs):
    w_refs = refs[: len(tags)]
    q_ref, kv_ref, x_v, a_v, w_v, x_sem, a_sem, w_sem = refs[len(tags) :]
    images, _, rows, _ = x_ref.shape
    copies = piece_copies(w_refs, [(0, t, a) for _, t, a in tags], parts, w_v, w_sem, 0)

    half = images // 2

    def loads(n):
        return [
            pltpu.make_async_copy(
                x_ref.at[n * half + k, images - 1],
                x_v.at[n, pl.ds(k * rows, rows)],
                x_sem.at[n * half + k],
            )
            for k in range(half)
        ] + [
            pltpu.make_async_copy(
                acc_ref.at[n * half + k], a_v.at[n, pl.ds(k * rows, rows)], a_sem.at[n * half + k]
            )
            for k in range(half)
        ]

    for n in range(2):
        for load in loads(n):
            load.start()
    for copy in copies:
        copy.wait()

    def block(n, carry):
        for load in loads(n):
            load.wait()
        got = a_v[n] + jnp.dot(x_v[n], w_v[...], preferred_element_type=jnp.float32)
        got = got.astype(jnp.bfloat16)
        own = pl.ds(pl.multiple_of(n * half * rows, 16), half * rows)
        for h in range(heads):
            at = 3 * HDIM * h
            q_ref[own, h * HDIM : (h + 1) * HDIM] = got[:, at : at + HDIM]
            kv_ref[own, 2 * h * HDIM : 2 * (h + 1) * HDIM] = got[:, at + HDIM : at + 3 * HDIM]
        return carry

    lax.fori_loop(0, 2, block, 0)


def project_late(normed, acc, pieces, parts):
    images, _, rows, span = normed.shape
    columns = pieces[0][3].shape[1]
    heads = columns // (3 * HDIM)
    tags = [(s, t, a) for s, t, a, _ in pieces]
    tokens = images * rows
    return pl.pallas_call(
        functools.partial(late_kernel, parts, heads, tags),
        in_specs=[ANY] * (2 + len(pieces)),
        out_specs=[VMEM, VMEM],
        out_shape=[
            jax.ShapeDtypeStruct((tokens, heads * HDIM), jnp.bfloat16),
            jax.ShapeDtypeStruct((tokens, 2 * heads * HDIM), jnp.bfloat16),
        ],
        scratch_shapes=[
            pltpu.VMEM((2, tokens // 2, span), jnp.bfloat16),
            pltpu.VMEM((2, tokens // 2, columns), jnp.float32),
            pltpu.VMEM((span, columns), jnp.bfloat16),
            pltpu.SemaphoreType.DMA((images,)),
            pltpu.SemaphoreType.DMA((images,)),
            pltpu.SemaphoreType.DMA((parts,)),
        ],
        cost_estimate=cost(2 * tokens * span * columns, 8 * tokens * columns),
        name="late",
        compiler_params=pltpu.CompilerParams(vmem_limit_bytes=24 << 20),
    )(normed, acc, *[w for _, _, _, w in pieces])


def attend_kernel(first, slots, heads, q_ref, *refs):
    kv_refs, out_refs = refs[:-slots], refs[-slots:]
    rows = out_refs[0].shape[0]
    scale = HDIM ** (-0.5) * math.log2(math.e)
    own = slice(first * rows, (first + slots) * rows)
    for h in range(heads):
        query = q_ref[own, h * HDIM : (h + 1) * HDIM]
        scores = [
            lax.dot_general(
                query,
                ref[:, 2 * h * HDIM : (2 * h + 1) * HDIM],
                (((1,), (1,)), ((), ())),
                preferred_element_type=jnp.float32,
            )
            for ref in kv_refs
        ]
        peak = functools.reduce(jnp.maximum, [jnp.max(s, axis=-1, keepdims=True) for s in scores])
        peak = peak * scale
        both = 0.0
        for s, ref in zip(scores, kv_refs):
            expo = jnp.exp2(s * scale - peak).astype(jnp.bfloat16)
            value = ref[:, (2 * h + 1) * HDIM : 2 * (h + 1) * HDIM]
            value = jnp.concatenate([value, jnp.ones_like(value)], axis=1)
            both += jnp.dot(expo, value, preferred_element_type=jnp.float32)
        got = (both[:, :HDIM] / both[:, HDIM:]).astype(jnp.bfloat16)
        for m in range(slots):
            out_refs[m][:, h * HDIM : (h + 1) * HDIM] = got[m * rows : (m + 1) * rows]


def attend(query, pairs, images, first, slots):
    tokens, wide = query.shape
    rows, heads = tokens // images, wide // HDIM
    keys = tokens * len(pairs)
    return pl.pallas_call(
        functools.partial(attend_kernel, first, slots, heads),
        in_specs=[VMEM] * (1 + len(pairs)),
        out_specs=[VMEM] * slots,
        out_shape=[jax.ShapeDtypeStruct((rows, wide), jnp.bfloat16)] * slots,
        cost_estimate=cost(
            8 * heads * slots * rows * keys * HDIM,
            4 * heads * HDIM * (tokens + keys),
            heads * slots * rows * keys,
        ),
        name="attend",
        compiler_params=pltpu.CompilerParams(vmem_limit_bytes=32 << 20),
    )(query, *pairs)


def out_kernel(parts, turns, tags, w_tags, last, base_ref, *refs):
    w_refs, refs = refs[: len(w_tags)], refs[len(w_tags) :]
    o_refs = refs[: len(tags)]
    outs = refs[len(tags) : len(tags) + (1 if last else 2)]
    o_v, w_v, b_v, r_v, o_sem, w_sem, b_sem, r_sem, k_sem = refs[len(tags) + len(outs) :]
    me, col = lax.axis_index("row"), lax.axis_index("col")
    images, rows, columns = base_ref.shape
    image, part = col // parts, col % parts
    half = images // 2
    deep = w_v.shape[0]
    spots = [(image + k) % images for k in turns]
    cuts = column_cuts(columns)
    heads = []
    for n, (chunk, mask, block) in enumerate(tags):
        if last:
            continue
        size, width = o_refs[n].shape
        per = parts * w_refs[0].shape[0] // (CHUNKS * width)
        other = me ^ mask
        slot = (image + images - other // per) % images
        at = pl.multiple_of(((slot * per + other % per) * CHUNKS + chunk) * width, 128)
        to = o_v.at[pl.ds(block * rows, size), pl.ds(at, width)]
        heads.append(pltpu.make_async_copy(o_refs[n], to, o_sem.at[n]))
    weights = []
    for m, (begin, size) in enumerate(cuts):
        for n, (step, turn) in enumerate(w_tags):
            depth = w_refs[n].shape[0]
            first = 0 if last else step * parts * depth
            at = pl.multiple_of(first + (part + parts - turn) % parts * depth, 16)
            span = pl.ds(begin, size)
            weights.append(
                pltpu.make_async_copy(
                    w_refs[n].at[:, span], w_v.at[pl.ds(at, depth), span], w_sem.at[m, n]
                )
            )
    bases = []
    if not last:
        bases = [
            pltpu.make_async_copy(base_ref.at[spot], b_v.at[n], b_sem.at[n])
            for n, spot in enumerate(spots)
        ]
    held, added = (o_refs[0], base_ref) if last else (o_v, b_v)
    per = len(w_tags)
    for copy in heads + weights[:per] + bases + weights[per:]:
        copy.start()
    for copy in heads:
        copy.wait()
    keep = None
    if not last:
        keep = pltpu.make_async_copy(
            o_v.at[:, pl.ds(deep, o_v.shape[1] - deep)], outs[1], k_sem.at[0]
        )
        keep.start()

    def store(m, n, spot):
        span = pl.ds(*cuts[m])
        to = spot if last else n
        return pltpu.make_async_copy(r_v.at[n, :, span], outs[0].at[to, :, span], r_sem.at[m, n])

    for m, (begin, size) in enumerate(cuts):
        for copy in weights[m * per : (m + 1) * per]:
            copy.wait()
        if m == 0:
            for copy in bases:
                copy.wait()

        def body(block, carry, m=m, begin=begin, size=size):
            at = pl.ds(pl.multiple_of(block * half * rows, 16), half * rows)
            got = jnp.dot(
                held[at, :deep], w_v[:, begin : begin + size], preferred_element_type=jnp.float32
            )
            for k in range(half):
                n = block * half + k
                mine = got[k * rows : (k + 1) * rows]
                r_v[n, :, begin : begin + size] = (
                    added[n, :, begin : begin + size].astype(jnp.float32) + mine
                ).astype(r_v.dtype)
                store(m, n, jnp.where(block == 0, spots[k], spots[half + k])).start()
            return carry

        lax.fori_loop(0, 2, body, 0)
    for m in range(len(cuts)):
        for n, spot in enumerate(spots):
            store(m, n, spot).wait()
    if keep is not None:
        keep.wait()


def column_cuts(columns):
    first = -(-columns // 512) * 256
    return ((0, first), (first, columns - first))


def project_out(base, w_pieces, pieces, parts, turns, last):
    tags = [(chunk, m, block) for chunk, m, block, _ in pieces]
    w_tags = [(s, t) for s, t, _ in w_pieces]
    images, rows, columns = base.shape
    depth = w_pieces[0][2].shape[0]
    deep = len(w_pieces) * depth
    wide = deep if last else deep + parts * depth
    cuts = len(column_cuts(columns))
    kind = jnp.bfloat16 if last else jnp.float32
    tokens = images * rows
    shapes = [jax.ShapeDtypeStruct(base.shape, kind)]
    if not last:
        shapes.append(jax.ShapeDtypeStruct((tokens, wide - deep), jnp.bfloat16))
    return pl.pallas_call(
        functools.partial(out_kernel, parts, turns, tags, w_tags, last),
        in_specs=[VMEM if last else ANY]
        + [ANY] * len(w_tags)
        + [VMEM if last else ANY] * len(tags),
        out_specs=[ANY] * len(shapes),
        out_shape=shapes,
        scratch_shapes=[
            pltpu.VMEM((16, 128) if last else (tokens, wide), jnp.bfloat16),
            pltpu.VMEM((deep, columns), jnp.bfloat16),
            pltpu.VMEM((1, 8, 128) if last else base.shape, base.dtype),
            pltpu.VMEM(base.shape, kind),
            pltpu.SemaphoreType.DMA((len(tags),)),
            pltpu.SemaphoreType.DMA((cuts, len(w_tags))),
            pltpu.SemaphoreType.DMA((images,)),
            pltpu.SemaphoreType.DMA((cuts, images)),
            pltpu.SemaphoreType.DMA((1,)),
        ],
        cost_estimate=cost(2 * tokens * columns * deep, 8 * tokens * columns),
        name="out",
        compiler_params=pltpu.CompilerParams(vmem_limit_bytes=28 << 20),
    )(base, *[w for _, _, w in w_pieces], *[o for _, _, _, o in pieces])


def local(pixels_tokens, ln_gain, ln_bias, w_qkv, w_out):
    images, _, _ = pixels_tokens.shape
    row_count = lax.axis_size("row")
    col_count = lax.axis_size("col")
    parts = col_count // images
    head_row = w_qkv.shape[1] // (3 * HDIM)
    heads = head_row // CHUNKS
    image = lax.axis_index("col") // parts
    dims = [1 << n for n in range(row_count.bit_length() - 1)]

    def around(value, step):
        if step % images == 0:
            return value
        return lax.ppermute(value, "col", ring(images, parts, step))

    def swaps(step, shard):
        return [(step, 0, shard)] + [
            (step, t, lax.ppermute(shard, "col", group(images, parts, t)))
            for t in range(1, parts)
        ]

    shifts = SLOTS(images)
    blocks = []
    for k in shifts:
        block = lax.dynamic_index_in_dim(pixels_tokens, (image + k) % images, 0, keepdims=False)
        blocks.append(around(block, k))
    normed = None
    for slot in NORMS(images):
        k = shifts[slot]
        turned = dims[k % len(dims) :] + dims[: k % len(dims)]
        pieces = spread(blocks[slot], row_count, turned)
        normed = normalize(slot, normed, pieces, ln_gain, ln_bias, images, parts)

    columns = heads * 3 * HDIM
    own = [(0, t, None, w) for _, t, w in swaps(0, w_qkv)]

    def arrive(slot, holders, value, moves):
        got = lax.ppermute(value, "col", hop(parts, moves))
        there = [(a, a) for a in (holders or range(images))]
        turned = [(slot, 0, holders, got)]
        for t in range(1, parts):
            perm = [
                (a * parts + p, a * parts + (p + t) % parts) for a, _ in there for p in range(parts)
            ]
            turned.append((slot, t, holders, lax.ppermute(got, "col", perm)))
        return got, turned

    results = []
    for j in range(CHUNKS):
        shard = w_qkv[:, j * columns : (j + 1) * columns]
        near, one = arrive(1, None, shard, PAIRS)
        across, two = arrive(2, MIDDLES, shard, MIDDLE)
        _, three = arrive(2, ENDS, across, OUTWARD)
        far, four = arrive(3, MIDDLES, near, MIDDLE)
        _, five = arrive(3, ENDS, far, OUTWARD)
        first = own + one + two + three
        acc = project_early(normed, first, j * columns, columns, parts)
        query, pair = project_late(normed, acc, four + five, parts)
        pairs = [pair] + [
            lax.ppermute(pair, "col", group(images, parts, t)) for t in range(1, parts)
        ]
        half = images // 2
        outs = []
        for n in range(2):
            mine = shifts[n * half : (n + 1) * half]
            got = attend(query, pairs, images, n * half, half)
            outs += [around(o, -k) for k, o in zip(mine, got)]
        if j + 1 < CHUNKS:
            pieces = []
            for n in range(2):
                joined = jnp.concatenate(outs[n * half : (n + 1) * half], axis=0)
                turned = dims[n:] + dims[:n]
                pieces += [(n * half, spread(joined, row_count, turned))]
            results.append(pieces)
            continue
        pieces = []
        for n, (k, o) in enumerate(zip(shifts, outs)):
            turned = dims[n % len(dims) :] + dims[: n % len(dims)]
            pieces.append((n, spread(o, row_count, turned)))
        results.append(pieces)

    shard, out_pieces = w_out, []
    for step in range(images):
        out_pieces += swaps(step, shard)
        if step + 1 < images:
            shard = around(shard, 1)
    pieces = [
        (j, m, n, o) for j in range(CHUNKS) for n, got in results[j] for m, o in got
    ]
    split = len(out_pieces) - parts
    total, rest = project_out(pixels_tokens, out_pieces[:split], pieces, parts, shifts, False)
    pieces = [(0, 0, 0, rest)]
    return project_out(total, out_pieces[split:], pieces, parts, shifts, True)[0]


def SLOTS(images):
    return sorted(range(1, images), key=lambda k: (min(k, images - k), k)) + [0]


def NORMS(images):
    return [images - 1, 0] + list(range(images - 2, 0, -1))


def solution(mesh):
    in_specs = (P(None, "col", "row"), P(), P(), P("col", "row"), P("col", "row"))
    out_specs = P(None, "col", "row")

    def whole(pixels_tokens, *rest):
        step = jax.shard_map(
            local, mesh=mesh, in_specs=in_specs, out_specs=out_specs, check_vma=False
        )
        return step(pixels_tokens, *rest)

    return whole
```

```python
import functools
import math

import jax
import jax.numpy as jnp
from jax import lax
from jax.experimental import pallas as pl
from jax.experimental.pallas import tpu as pltpu
from jax.sharding import PartitionSpec as P

HDIM = 128
CHUNKS = 2
ANY = pl.BlockSpec(memory_space=pl.ANY)
VMEM = pl.BlockSpec(memory_space=pltpu.VMEM)


def ring(images, parts, step):
    return [
        (a * parts + b, ((a + step) % images) * parts + b)
        for a in range(images)
        for b in range(parts)
    ]


def group(images, parts, step):
    return [
        (a * parts + b, a * parts + (b + step) % parts)
        for a in range(images)
        for b in range(parts)
    ]


def tile_of(rows, limit):
    return max(t for t in range(16, limit + 1, 16) if rows % t == 0)


def cost(flops, moved, exps=0):
    return pl.CostEstimate(flops=flops, bytes_accessed=moved, transcendentals=exps)


def spread(block, rows, dims):
    pieces, n = [(0, block)], 0
    for d in dims:
        perm = [(a, a ^ d) for a in range(rows)]
        for m, b in list(pieces):
            pieces.append((m ^ d, lax.ppermute(b, "row", perm)))
            n += 1
    return pieces


def source_of(image, slot):
    table = ((0, 1, 2, 3), (1, 0, 2, 3), (2, 3, 1, 0), (3, 2, 1, 0))
    return sum(jnp.where(image == a, row[slot], 0) for a, row in enumerate(table))


def slot_of(image, source):
    return sum(jnp.where(source_of(image, slot) == source, slot, 0) for slot in range(4))


PAIRS = ((0, 1), (1, 0), (2, 3), (3, 2))
MIDDLE = ((1, 2), (2, 1))
OUTWARD = ((1, 0), (2, 3))
MIDDLES, ENDS = (1, 2), (0, 3)


def hop(parts, moves):
    return [(a * parts + p, b * parts + p) for a, b in moves for p in range(parts)]


def norm_kernel(masks, parts, gain_ref, bias_ref, *refs):
    pieces, out_ref = refs[: len(masks)], refs[-1]
    me = lax.axis_index("row")
    image = lax.axis_index("col") // parts
    width = pieces[0].shape[1]
    span = out_ref.shape[3]
    grain = min(width, span)
    total = width * len(pieces)
    floats = [ref[...].astype(jnp.float32) for ref in pieces]
    center = sum(jnp.sum(f, axis=-1, keepdims=True) for f in floats) / total
    floats = [f - center for f in floats]
    scatter = sum(jnp.sum(f * f, axis=-1, keepdims=True) for f in floats) / total
    scale = lax.rsqrt(scatter + 1e-06)
    for mask, f in zip(masks, floats):
        for part in range(width // grain):
            first = (me ^ mask) * width + part * grain
            at = pl.ds(pl.multiple_of(first, 128), grain)
            slot = slot_of(image, first // span)
            to = pl.ds(pl.multiple_of(first % span, 128), grain)
            value = f[:, part * grain : (part + 1) * grain] * scale
            out_ref[0, slot, :, to] = (value * gain_ref[:, at] + bias_ref[:, at]).astype(
                out_ref.dtype
            )


def normalize(k, held, pieces, gain, bias, images, parts):
    masks = [m for m, _ in pieces]
    rows, width = pieces[0][1].shape
    total = width * len(pieces)
    tile = tile_of(rows, 48)
    shape = (images, images, rows, total // images)
    whole = pl.BlockSpec((1, total), lambda t: (0, 0))
    extra = [] if held is None else [held]
    return pl.pallas_call(
        functools.partial(norm_kernel, masks, parts),
        grid=(rows // tile,),
        in_specs=[whole, whole]
        + [pl.BlockSpec((tile, width), lambda t: (t, 0))] * len(pieces)
        + [ANY] * len(extra),
        out_specs=pl.BlockSpec((1, images, tile, total // images), lambda t: (k, 0, t, 0)),
        out_shape=jax.ShapeDtypeStruct(shape, jnp.bfloat16),
        input_output_aliases={2 + len(pieces): 0} if extra else {},
        cost_estimate=cost(8 * rows * total, 4 * rows * total, rows),
        name="norm",
        compiler_params=pltpu.CompilerParams(vmem_limit_bytes=16 << 20),
    )(gain[None], bias[None], *[b for _, b in pieces], *extra)


def piece_copies(w_refs, tags, parts, w_v, sems, first):
    image, part = lax.axis_index("col") // parts, lax.axis_index("col") % parts
    columns = w_v.shape[1]
    waits = {}
    for ref, (slot, turn, holders) in zip(w_refs, tags):
        depth, wide = ref.shape
        at = pl.multiple_of(((part + parts - turn) % parts) * depth, 16)
        source = ref.at[:, pl.ds(first, columns)] if wide > columns else ref
        to = w_v.at[pl.ds(slot * parts * depth + at, depth)]
        copy = pltpu.make_async_copy(source, to, sems.at[slot * parts + turn])
        waits[slot, turn] = copy
        if holders is None:
            copy.start()
        else:
            held = functools.reduce(jnp.logical_or, [image == a for a in holders])
            pl.when(held)(copy.start)
    return list(waits.values())


def early_kernel(steps, parts, tags, first, x_ref, *refs):
    w_refs = refs[: len(tags)]
    out_ref, x_v, w_v, o_v, x_sem, w_sem, o_sem = refs[len(tags) :]
    images, _, _, span = x_ref.shape

    def load(k, s):
        to = x_v.at[k, :, pl.ds(s * span, span)]
        return pltpu.make_async_copy(x_ref.at[k, s], to, x_sem.at[k, s])

    def store(k):
        return pltpu.make_async_copy(o_v.at[k], out_ref.at[k], o_sem.at[k])

    copies = piece_copies(w_refs, tags, parts, w_v, w_sem, first)
    for s in range(steps):
        load(0, s).start()
    for copy in copies:
        copy.wait()

    def block(k, carry):
        for s in range(steps):
            load(k, s).wait()

        @pl.when(k + 1 < images)
        def _():
            for s in range(steps):
                load(k + 1, s).start()

        o_v[k] = jnp.dot(x_v[k], w_v[...], preferred_element_type=jnp.float32)
        store(k).start()
        return carry

    lax.fori_loop(0, images, block, 0)
    for k in range(images):
        store(k).wait()


def project_early(normed, pieces, first, columns, parts):
    images, _, rows, span = normed.shape
    tags = [(s, t, a) for s, t, a, _ in pieces]
    steps = images - 1
    tokens = images * rows
    shape = (images, rows, columns)
    return pl.pallas_call(
        functools.partial(early_kernel, steps, parts, tags, first),
        in_specs=[ANY] * (1 + len(pieces)),
        out_specs=ANY,
        out_shape=jax.ShapeDtypeStruct(shape, jnp.float32),
        scratch_shapes=[
            pltpu.VMEM((images, rows, steps * span), jnp.bfloat16),
            pltpu.VMEM((steps * span, columns), jnp.bfloat16),
            pltpu.VMEM(shape, jnp.float32),
            pltpu.SemaphoreType.DMA((images, steps)),
            pltpu.SemaphoreType.DMA((steps * parts,)),
            pltpu.SemaphoreType.DMA((images,)),
        ],
        cost_estimate=cost(2 * tokens * steps * span * columns, 2 * tokens * span * steps),
        name="early",
        compiler_params=pltpu.CompilerParams(vmem_limit_bytes=30 << 20),
    )(normed, *[w for _, _, _, w in pieces])


def late_kernel(parts, heads, tags, x_ref, acc_ref, *refs):
    w_refs = refs[: len(tags)]
    q_ref, kv_ref, x_v, a_v, w_v, x_sem, a_sem, w_sem = refs[len(tags) :]
    images, _, rows, _ = x_ref.shape
    copies = piece_copies(w_refs, [(0, t, a) for _, t, a in tags], parts, w_v, w_sem, 0)

    half = images // 2

    def loads(n):
        return [
            pltpu.make_async_copy(
                x_ref.at[n * half + k, images - 1],
                x_v.at[n, pl.ds(k * rows, rows)],
                x_sem.at[n * half + k],
            )
            for k in range(half)
        ] + [
            pltpu.make_async_copy(
                acc_ref.at[n * half + k], a_v.at[n, pl.ds(k * rows, rows)], a_sem.at[n * half + k]
            )
            for k in range(half)
        ]

    for n in range(2):
        for load in loads(n):
            load.start()
    for copy in copies:
        copy.wait()

    def block(n, carry):
        for load in loads(n):
            load.wait()
        got = a_v[n] + jnp.dot(x_v[n], w_v[...], preferred_element_type=jnp.float32)
        got = got.astype(jnp.bfloat16)
        own = pl.ds(pl.multiple_of(n * half * rows, 16), half * rows)
        for h in range(heads):
            at = 3 * HDIM * h
            q_ref[own, h * HDIM : (h + 1) * HDIM] = got[:, at : at + HDIM]
            kv_ref[own, 2 * h * HDIM : 2 * (h + 1) * HDIM] = got[:, at + HDIM : at + 3 * HDIM]
        return carry

    lax.fori_loop(0, 2, block, 0)


def project_late(normed, acc, pieces, parts):
    images, _, rows, span = normed.shape
    columns = pieces[0][3].shape[1]
    heads = columns // (3 * HDIM)
    tags = [(s, t, a) for s, t, a, _ in pieces]
    tokens = images * rows
    return pl.pallas_call(
        functools.partial(late_kernel, parts, heads, tags),
        in_specs=[ANY] * (2 + len(pieces)),
        out_specs=[VMEM, VMEM],
        out_shape=[
            jax.ShapeDtypeStruct((tokens, heads * HDIM), jnp.bfloat16),
            jax.ShapeDtypeStruct((tokens, 2 * heads * HDIM), jnp.bfloat16),
        ],
        scratch_shapes=[
            pltpu.VMEM((2, tokens // 2, span), jnp.bfloat16),
            pltpu.VMEM((2, tokens // 2, columns), jnp.float32),
            pltpu.VMEM((span, columns), jnp.bfloat16),
            pltpu.SemaphoreType.DMA((images,)),
            pltpu.SemaphoreType.DMA((images,)),
            pltpu.SemaphoreType.DMA((parts,)),
        ],
        cost_estimate=cost(2 * tokens * span * columns, 8 * tokens * columns),
        name="late",
        compiler_params=pltpu.CompilerParams(vmem_limit_bytes=24 << 20),
    )(normed, acc, *[w for _, _, _, w in pieces])


def attend_kernel(first, slots, heads, q_ref, *refs):
    kv_refs, out_refs = refs[:-slots], refs[-slots:]
    rows = out_refs[0].shape[0]
    scale = HDIM ** (-0.5) * math.log2(math.e)
    own = slice(first * rows, (first + slots) * rows)
    for h in range(heads):
        query = q_ref[own, h * HDIM : (h + 1) * HDIM]
        scores = [
            lax.dot_general(
                query,
                ref[:, 2 * h * HDIM : (2 * h + 1) * HDIM],
                (((1,), (1,)), ((), ())),
                preferred_element_type=jnp.float32,
            )
            for ref in kv_refs
        ]
        peak = functools.reduce(jnp.maximum, [jnp.max(s, axis=-1, keepdims=True) for s in scores])
        peak = peak * scale
        both = 0.0
        for s, ref in zip(scores, kv_refs):
            expo = jnp.exp2(s * scale - peak).astype(jnp.bfloat16)
            value = ref[:, (2 * h + 1) * HDIM : 2 * (h + 1) * HDIM]
            value = jnp.concatenate([value, jnp.ones_like(value)], axis=1)
            both += jnp.dot(expo, value, preferred_element_type=jnp.float32)
        got = (both[:, :HDIM] / both[:, HDIM:]).astype(jnp.bfloat16)
        for m in range(slots):
            out_refs[m][:, h * HDIM : (h + 1) * HDIM] = got[m * rows : (m + 1) * rows]


def attend(query, pairs, images, first, slots):
    tokens, wide = query.shape
    rows, heads = tokens // images, wide // HDIM
    keys = tokens * len(pairs)
    return pl.pallas_call(
        functools.partial(attend_kernel, first, slots, heads),
        in_specs=[VMEM] * (1 + len(pairs)),
        out_specs=[VMEM] * slots,
        out_shape=[jax.ShapeDtypeStruct((rows, wide), jnp.bfloat16)] * slots,
        cost_estimate=cost(
            8 * heads * slots * rows * keys * HDIM,
            4 * heads * HDIM * (tokens + keys),
            heads * slots * rows * keys,
        ),
        name="attend",
        compiler_params=pltpu.CompilerParams(vmem_limit_bytes=32 << 20),
    )(query, *pairs)


def out_kernel(parts, turns, tags, w_tags, last, base_ref, *refs):
    w_refs, refs = refs[: len(w_tags)], refs[len(w_tags) :]
    o_refs = refs[: len(tags)]
    outs = refs[len(tags) : len(tags) + (1 if last else 2)]
    o_v, w_v, b_v, r_v, o_sem, w_sem, b_sem, r_sem, k_sem = refs[len(tags) + len(outs) :]
    me, col = lax.axis_index("row"), lax.axis_index("col")
    images, rows, columns = base_ref.shape
    image, part = col // parts, col % parts
    half = images // 2
    deep = w_v.shape[0]
    spots = [(image + k) % images for k in turns]
    cuts = column_cuts(columns)
    heads = []
    for n, (chunk, mask, block) in enumerate(tags):
        if last:
            continue
        size, width = o_refs[n].shape
        per = parts * w_refs[0].shape[0] // (CHUNKS * width)
        other = me ^ mask
        slot = (image + images - other // per) % images
        at = pl.multiple_of(((slot * per + other % per) * CHUNKS + chunk) * width, 128)
        to = o_v.at[pl.ds(block * rows, size), pl.ds(at, width)]
        heads.append(pltpu.make_async_copy(o_refs[n], to, o_sem.at[n]))
    weights = []
    for m, (begin, size) in enumerate(cuts):
        for n, (step, turn) in enumerate(w_tags):
            depth = w_refs[n].shape[0]
            first = 0 if last else step * parts * depth
            at = pl.multiple_of(first + (part + parts - turn) % parts * depth, 16)
            span = pl.ds(begin, size)
            weights.append(
                pltpu.make_async_copy(
                    w_refs[n].at[:, span], w_v.at[pl.ds(at, depth), span], w_sem.at[m, n]
                )
            )
    bases = []
    if not last:
        bases = [
            pltpu.make_async_copy(base_ref.at[spot], b_v.at[n], b_sem.at[n])
            for n, spot in enumerate(spots)
        ]
    held, added = (o_refs[0], base_ref) if last else (o_v, b_v)
    per = len(w_tags)
    for copy in heads + weights[:per] + bases + weights[per:]:
        copy.start()
    for copy in heads:
        copy.wait()
    keep = None
    if not last:
        keep = pltpu.make_async_copy(
            o_v.at[:, pl.ds(deep, o_v.shape[1] - deep)], outs[1], k_sem.at[0]
        )
        keep.start()

    def store(m, n, spot):
        span = pl.ds(*cuts[m])
        to = spot if last else n
        return pltpu.make_async_copy(r_v.at[n, :, span], outs[0].at[to, :, span], r_sem.at[m, n])

    for m, (begin, size) in enumerate(cuts):
        for copy in weights[m * per : (m + 1) * per]:
            copy.wait()
        if m == 0:
            for copy in bases:
                copy.wait()

        def body(block, carry, m=m, begin=begin, size=size):
            at = pl.ds(pl.multiple_of(block * half * rows, 16), half * rows)
            got = jnp.dot(
                held[at, :deep], w_v[:, begin : begin + size], preferred_element_type=jnp.float32
            )
            for k in range(half):
                n = block * half + k
                mine = got[k * rows : (k + 1) * rows]
                target = r_v if last else outs[0]
                target[n, :, begin : begin + size] = (
                    added[n, :, begin : begin + size].astype(jnp.float32) + mine
                ).astype(target.dtype)
                if last:
                    store(m, n, jnp.where(block == 0, spots[k], spots[half + k])).start()
            return carry

        lax.fori_loop(0, 2, body, 0)
    if last:
        for m in range(len(cuts)):
            for n, spot in enumerate(spots):
                store(m, n, spot).wait()
    if keep is not None:
        keep.wait()


def column_cuts(columns):
    first = -(-columns // 512) * 256
    return ((0, first), (first, columns - first))


def project_out(base, w_pieces, pieces, parts, turns, last):
    tags = [(chunk, m, block) for chunk, m, block, _ in pieces]
    w_tags = [(s, t) for s, t, _ in w_pieces]
    images, rows, columns = base.shape
    depth = w_pieces[0][2].shape[0]
    deep = len(w_pieces) * depth
    wide = deep if last else deep + parts * depth
    cuts = len(column_cuts(columns))
    kind = jnp.bfloat16 if last else jnp.float32
    tokens = images * rows
    shapes = [jax.ShapeDtypeStruct(base.shape, kind)]
    if not last:
        shapes.append(jax.ShapeDtypeStruct((tokens, wide - deep), jnp.bfloat16))
    return pl.pallas_call(
        functools.partial(out_kernel, parts, turns, tags, w_tags, last),
        in_specs=[VMEM if last else ANY]
        + [ANY] * len(w_tags)
        + [VMEM if last else ANY] * len(tags),
        out_specs=[ANY] if last else [VMEM, ANY],
        out_shape=shapes,
        scratch_shapes=[
            pltpu.VMEM((16, 128) if last else (tokens, wide), jnp.bfloat16),
            pltpu.VMEM((deep, columns), jnp.bfloat16),
            pltpu.VMEM((1, 8, 128) if last else base.shape, base.dtype),
            pltpu.VMEM(base.shape if last else (1, 8, 128), kind),
            pltpu.SemaphoreType.DMA((len(tags),)),
            pltpu.SemaphoreType.DMA((cuts, len(w_tags))),
            pltpu.SemaphoreType.DMA((images,)),
            pltpu.SemaphoreType.DMA((cuts, images)),
            pltpu.SemaphoreType.DMA((1,)),
        ],
        cost_estimate=cost(2 * tokens * columns * deep, 8 * tokens * columns),
        name="out",
        compiler_params=pltpu.CompilerParams(vmem_limit_bytes=28 << 20),
    )(base, *[w for _, _, w in w_pieces], *[o for _, _, _, o in pieces])


def local(pixels_tokens, ln_gain, ln_bias, w_qkv, w_out):
    images, _, _ = pixels_tokens.shape
    row_count = lax.axis_size("row")
    col_count = lax.axis_size("col")
    parts = col_count // images
    head_row = w_qkv.shape[1] // (3 * HDIM)
    heads = head_row // CHUNKS
    image = lax.axis_index("col") // parts
    dims = [1 << n for n in range(row_count.bit_length() - 1)]

    def around(value, step):
        if step % images == 0:
            return value
        return lax.ppermute(value, "col", ring(images, parts, step))

    def swaps(step, shard):
        return [(step, 0, shard)] + [
            (step, t, lax.ppermute(shard, "col", group(images, parts, t)))
            for t in range(1, parts)
        ]

    shifts = SLOTS(images)
    blocks = []
    for k in shifts:
        block = lax.dynamic_index_in_dim(pixels_tokens, (image + k) % images, 0, keepdims=False)
        blocks.append(around(block, k))
    normed = None
    for slot in NORMS(images):
        k = shifts[slot]
        turned = dims[k % len(dims) :] + dims[: k % len(dims)]
        pieces = spread(blocks[slot], row_count, turned)
        normed = normalize(slot, normed, pieces, ln_gain, ln_bias, images, parts)

    columns = heads * 3 * HDIM
    own = [(0, t, None, w) for _, t, w in swaps(0, w_qkv)]

    def arrive(slot, holders, value, moves):
        got = lax.ppermute(value, "col", hop(parts, moves))
        there = [(a, a) for a in (holders or range(images))]
        turned = [(slot, 0, holders, got)]
        for t in range(1, parts):
            perm = [
                (a * parts + p, a * parts + (p + t) % parts) for a, _ in there for p in range(parts)
            ]
            turned.append((slot, t, holders, lax.ppermute(got, "col", perm)))
        return got, turned

    results = []
    for j in range(CHUNKS):
        shard = w_qkv[:, j * columns : (j + 1) * columns]
        near, one = arrive(1, None, shard, PAIRS)
        across, two = arrive(2, MIDDLES, shard, MIDDLE)
        _, three = arrive(2, ENDS, across, OUTWARD)
        far, four = arrive(3, MIDDLES, near, MIDDLE)
        _, five = arrive(3, ENDS, far, OUTWARD)
        first = own + one + two + three
        acc = project_early(normed, first, j * columns, columns, parts)
        query, pair = project_late(normed, acc, four + five, parts)
        pairs = [pair] + [
            lax.ppermute(pair, "col", group(images, parts, t)) for t in range(1, parts)
        ]
        half = images // 2
        outs = []
        for n in range(2):
            mine = shifts[n * half : (n + 1) * half]
            got = attend(query, pairs, images, n * half, half)
            outs += [around(o, -k) for k, o in zip(mine, got)]
        if j + 1 < CHUNKS:
            pieces = []
            for n in range(2):
                joined = jnp.concatenate(outs[n * half : (n + 1) * half], axis=0)
                turned = dims[n:] + dims[:n]
                pieces += [(n * half, spread(joined, row_count, turned))]
            results.append(pieces)
            continue
        pieces = []
        for n, (k, o) in enumerate(zip(shifts, outs)):
            turned = dims[n % len(dims) :] + dims[: n % len(dims)]
            pieces.append((n, spread(o, row_count, turned)))
        results.append(pieces)

    shard, out_pieces = w_out, []
    for step in range(images):
        out_pieces += swaps(step, shard)
        if step + 1 < images:
            shard = around(shard, 1)
    pieces = [
        (j, m, n, o) for j in range(CHUNKS) for n, got in results[j] for m, o in got
    ]
    split = len(out_pieces) - parts
    total, rest = project_out(pixels_tokens, out_pieces[:split], pieces, parts, shifts, False)
    pieces = [(0, 0, 0, rest)]
    return project_out(total, out_pieces[split:], pieces, parts, shifts, True)[0]


def SLOTS(images):
    return sorted(range(1, images), key=lambda k: (min(k, images - k), k)) + [0]


def NORMS(images):
    return [images - 1, 0] + list(range(images - 2, 0, -1))


def solution(mesh):
    in_specs = (P(None, "col", "row"), P(), P(), P("col", "row"), P("col", "row"))
    out_specs = P(None, "col", "row")

    def whole(pixels_tokens, *rest):
        step = jax.shard_map(
            local, mesh=mesh, in_specs=in_specs, out_specs=out_specs, check_vma=False
        )
        return step(pixels_tokens, *rest)

    return whole
```
